32 devices in a mesh: chan: 8 (over z, y), tm: 4 (over x, core).
Axes of the slice: x: 2, y: 2, z: 4, core: 2. Of those that a mesh axis runs over, the one named last changes fastest.
Arguments:
- samples: float32 [256, 4096], P('chan', 'tm'), may hold values from -6 to 6
- thresholds: int32 [3, 6], replicated, may hold values from 8 to 48
- sources: int32 [64], replicated, may hold values from 0 to 255
Outputs:
- correlations: float32 [64, 256, 512], P(None, ('chan', 'tm'))
The draws below stay inside these ranges and needn't reach their ends.
Inputs may be any that keep to these rules, and one draw needn't show every extreme that they name: Channel numbers of the virtual sources; two may be equal.
All inputs are finite; a program needn't handle non-finite values.
Results may differ from the reference program's by a relative error of at most 0.0074.
Values may be sent and summed in bfloat16 or wider, within the bound.
A program may use at most 64 MiB of HBM per device.

```python
import math
import jax
import jax.numpy as jnp
from jax import lax

N = 1024
LEVELS = 3
SOURCES = 64
BINS = 512
LAGS = 512
CHANNELS = 256
WINDOWS = 4
TIME = 4096


def touch_ends(entries, key, low, largest):
    spot = [jax.random.randint(jax.random.fold_in(key, axis), (), 0, length) for axis, length in enumerate(entries.shape)]
    longest = entries.shape.index(max(entries.shape))
    beside = spot[:longest] + [(spot[longest] + 1) % entries.shape[longest]] + spot[longest + 1:]
    return entries.at[tuple(spot)].set(low).at[tuple(beside)].set(largest)


def level_of(own_key, shape, shards, smallest, high):
    loudness = 1.0
    for dim, parts in shards:
        heights = jax.random.uniform(jax.random.fold_in(jax.random.fold_in(own_key, 6), dim), (parts,), jnp.float32, smallest / len(shards), high / len(shards))
        loudness = loudness * jnp.repeat(jnp.exp(heights), shape[dim] // parts).reshape((-1,) + (1,) * (len(shape) - 1 - dim))
    return loudness


def noise(key, shape, spread, most, cuts=(), held_as=jnp.bfloat16):
    entries = spread * jax.random.normal(key, shape, jnp.float32)
    if cuts:
        entries = entries * level_of(key, shape, cuts, -0.22, 0.18)
    return jnp.clip(entries, -most, most).astype(held_as)


def setup_inputs(seed: int = 0) -> dict:
    key_list = jax.random.split(jax.random.key(seed), 4)
    samples = noise(key_list[0], (CHANNELS, TIME), 1.0, 6.0, ((0, 8), (1, 4)), jnp.float32)
    thresholds = touch_ends(jax.random.randint(key_list[1], (LEVELS, 6), 8, 49), jax.random.fold_in(key_list[1], 1), 8, 48).astype(jnp.int32)
    sources = touch_ends(jax.random.randint(key_list[2], (SOURCES,), 0, CHANNELS), jax.random.fold_in(key_list[2], 1), 0, CHANNELS - 1).astype(jnp.int32)
    return dict(samples=samples, thresholds=thresholds, sources=sources)


daubechies = [0.2303778133088964, 0.7148465705529155, 0.6308807679298587, -0.0279837694168599, -0.1870348117190931, 0.0308413818355607, 0.0328830116668852, -0.010597401785069]

def filter_bank():
    lowpass = list(daubechies)
    highpass = [(1.0 if tap_index % 2 == 0 else -1.0) * daubechies[7 - tap_index] for tap_index in range(8)]
    return [(lowpass, highpass), (lowpass[::-1], highpass[::-1])]

def analyse(extended, filter_taps, dimension, length):
    summed = filter_taps[0] * lax.slice_in_dim(extended, 0, length - 1, 2, dimension)
    for tap_index in range(1, 8):
        summed = summed + filter_taps[tap_index] * lax.slice_in_dim(extended, tap_index, tap_index + length - 1, 2, dimension)
    return summed

def synthesise(low_ext, high_ext, low_taps, high_taps, dimension, length):
    even_part = None
    odd_part = None
    for step_index in range(4):
        even_term = low_taps[2 * step_index + 1] * lax.slice_in_dim(low_ext, 3 - step_index, 3 - step_index + length, 1, dimension) + high_taps[2 * step_index + 1] * lax.slice_in_dim(high_ext, 3 - step_index, 3 - step_index + length, 1, dimension)
        odd_term = low_taps[2 * step_index] * lax.slice_in_dim(low_ext, 4 - step_index, 4 - step_index + length, 1, dimension) + high_taps[2 * step_index] * lax.slice_in_dim(high_ext, 4 - step_index, 4 - step_index + length, 1, dimension)
        even_part = even_term if even_part is None else even_part + even_term
        odd_part = odd_term if odd_part is None else odd_part + odd_term
    woven = jnp.stack([even_part, odd_part], dimension + 1)
    new_shape = list(even_part.shape)
    new_shape[dimension] = 2 * new_shape[dimension]
    return woven.reshape(new_shape)

def shrink_band(band_aa, band_ab, band_ba, band_bb, cutoff_one, cutoff_two):
    root_half = 1.0 / math.sqrt(2.0)
    real_one = (band_aa - band_bb) * root_half
    imaginary_one = (band_ab + band_ba) * root_half
    real_two = (band_aa + band_bb) * root_half
    imaginary_two = (band_ab - band_ba) * root_half
    magnitude_one = jnp.sqrt(real_one * real_one + imaginary_one * imaginary_one)
    magnitude_two = jnp.sqrt(real_two * real_two + imaginary_two * imaginary_two)
    factor_one = jnp.maximum(magnitude_one - cutoff_one, 0.0) / jnp.maximum(magnitude_one, cutoff_one)
    factor_two = jnp.maximum(magnitude_two - cutoff_two, 0.0) / jnp.maximum(magnitude_two, cutoff_two)
    real_one = real_one * factor_one
    imaginary_one = imaginary_one * factor_one
    real_two = real_two * factor_two
    imaginary_two = imaginary_two * factor_two
    return ((real_one + real_two) * root_half, (imaginary_one + imaginary_two) * root_half, (imaginary_one - imaginary_two) * root_half, (real_two - real_one) * root_half)

def shrink_level(bands, thresholds, level_index):
    cutoffs = thresholds[level_index].astype(jnp.float32) / 32.0
    result = [[None, None, None] for tree_index in range(4)]
    for orient in range(3):
        shrunk = shrink_band(bands[0][orient + 1], bands[1][orient + 1], bands[2][orient + 1], bands[3][orient + 1], cutoffs[2 * orient], cutoffs[2 * orient + 1])
        for tree_index in range(4):
            result[tree_index][orient] = shrunk[tree_index]
    return result

def wrap_extend(values, width, dimension):
    size_along = values.shape[dimension]
    head_part = lax.slice_in_dim(values, size_along - width, size_along, 1, dimension)
    tail_part = lax.slice_in_dim(values, 0, width, 1, dimension)
    return jnp.concatenate([head_part, values, tail_part], dimension)

def denoise(samples, thresholds):
    bank = filter_bank()
    tree_list = [(0, 0), (0, 1), (1, 0), (1, 1)]
    current = [samples, samples, samples, samples]
    saved = []
    for level_index in range(LEVELS):
        bands = []
        for tree_index in range(4):
            chan_tree, time_tree = tree_list[tree_index]
            source_band = current[tree_index]
            extended = wrap_extend(source_band, 3, 1)
            time_low = analyse(extended, bank[time_tree][0], 1, source_band.shape[1])
            time_high = analyse(extended, bank[time_tree][1], 1, source_band.shape[1])
            low_ext = wrap_extend(time_low, 3, 0)
            high_ext = wrap_extend(time_high, 3, 0)
            row_count = source_band.shape[0]
            bands.append([analyse(low_ext, bank[chan_tree][0], 0, row_count), analyse(high_ext, bank[chan_tree][0], 0, row_count), analyse(low_ext, bank[chan_tree][1], 0, row_count), analyse(high_ext, bank[chan_tree][1], 0, row_count)])
        current = [band_set[0] for band_set in bands]
        saved.append(shrink_level(bands, thresholds, level_index))
    for level_index in reversed(range(LEVELS)):
        details = saved[level_index]
        rebuilt = []
        for tree_index in range(4):
            chan_tree, time_tree = tree_list[tree_index]
            lowband = current[tree_index]
            band_lh, band_hl, band_hh = details[tree_index]
            time_low = synthesise(wrap_extend(lowband, 2, 0), wrap_extend(band_hl, 2, 0), bank[chan_tree][0], bank[chan_tree][1], 0, lowband.shape[0])
            time_high = synthesise(wrap_extend(band_lh, 2, 0), wrap_extend(band_hh, 2, 0), bank[chan_tree][0], bank[chan_tree][1], 0, lowband.shape[0])
            rebuilt.append(synthesise(wrap_extend(time_low, 2, 1), wrap_extend(time_high, 2, 1), bank[time_tree][0], bank[time_tree][1], 1, time_low.shape[1]))
        current = rebuilt
    return (0.25 * (current[0] + current[1] + current[2] + current[3])).astype(jnp.bfloat16)

def dft_table():
    sample_index = jnp.arange(N, dtype=jnp.int32)
    frequency = jnp.arange(BINS, dtype=jnp.int32)
    phases = (sample_index[:, None] * frequency[None, :] % N).astype(jnp.float32) * (2.0 * math.pi / N)
    return jnp.concatenate([jnp.cos(phases), -jnp.sin(phases)], 1).astype(jnp.bfloat16)

def lag_table(window_count):
    frequency = jnp.arange(BINS, dtype=jnp.int32)
    shifts = jnp.arange(LAGS, dtype=jnp.int32) - LAGS // 2
    phases = jnp.mod(frequency[:, None] * shifts[None, :], N).astype(jnp.float32) * (2.0 * math.pi / N)
    weights = jnp.where(frequency == 0, 1.0, 2.0).astype(jnp.float32)[:, None] / math.sqrt(window_count * N)
    return jnp.concatenate([weights * jnp.cos(phases), -weights * jnp.sin(phases)], 0).astype(jnp.bfloat16)

def correlate(source_block, first_recv, second_recv, table):
    half_width = source_block.shape[-1] // 2
    stacked = jnp.concatenate([source_block[:, :, :half_width], source_block[:, :, half_width:]], 1).astype(jnp.float32)
    cross_real = jnp.einsum('skf,rkf->srf', stacked, first_recv)
    cross_imag = jnp.einsum('skf,rkf->srf', stacked, second_recv)
    cross_spec = lax.optimization_barrier(jnp.concatenate([cross_real, cross_imag], -1).astype(jnp.bfloat16)).astype(jnp.float32)
    flat = cross_spec.reshape(-1, cross_spec.shape[-1])
    result = jnp.dot(flat, table.astype(jnp.float32), preferred_element_type=jnp.float32)
    return result.reshape(source_block.shape[0], first_recv.shape[0], table.shape[1])

def reference(samples, thresholds, sources):
    denoised = lax.optimization_barrier(denoise(samples, thresholds)).astype(jnp.float32)
    spectra = jnp.dot(denoised.reshape(-1, N), dft_table().astype(jnp.float32), preferred_element_type=jnp.float32)
    whitened = spectra * lax.rsqrt(lax.optimization_barrier(jnp.mean(spectra * spectra, axis=1, keepdims=True)) + 1e-05)
    whitened = lax.optimization_barrier(whitened.astype(jnp.bfloat16)).astype(jnp.float32)
    whitened = whitened.reshape(CHANNELS, WINDOWS, N)
    picked = whitened[sources.astype(jnp.int32)]
    recv_real = whitened[:, :, :BINS]
    recv_imag = whitened[:, :, BINS:]
    first_recv = jnp.concatenate([recv_real, recv_imag], 1)
    second_recv = jnp.concatenate([-recv_imag, recv_real], 1)
    table = lag_table(WINDOWS)
    blocks = picked.reshape(SOURCES // 8, 8, WINDOWS, N)
    result = lax.map(lambda block_item: correlate(block_item, first_recv, second_recv, table), blocks)
    return result.reshape(SOURCES, CHANNELS, LAGS)
```

```python
import math

import jax
import jax.numpy as jnp
import numpy as np
from jax import lax
from jax.experimental import pallas as pl
from jax.experimental.pallas import tpu as pltpu
from jax.sharding import PartitionSpec as P

N = 1024
LEVELS = 3
BINS = 512
LAGS = 512
BLOCK = 128
HALF = 64
MESH = pl.DeviceIdType.MESH

daubechies = [
    0.2303778133088964,
    0.7148465705529155,
    0.6308807679298587,
    -0.0279837694168599,
    -0.1870348117190931,
    0.0308413818355607,
    0.0328830116668852,
    -0.010597401785069,
]


def filter_bank():
    lowpass = list(daubechies)
    highpass = [(1.0 if k % 2 == 0 else -1.0) * daubechies[7 - k] for k in range(8)]
    return [(lowpass, highpass), (lowpass[::-1], highpass[::-1])]


def bank_matrix(length):
    half = length // 2
    out = np.zeros((2, 2, half, length))
    rows = np.arange(half)
    for tree, pair in enumerate(filter_bank()):
        for band, taps in enumerate(pair):
            for k in range(8):
                np.add.at(out[tree, band], (rows, (2 * rows + k - 3) % length), taps[k])
    return out.reshape(2, length, length)


def halves(matrix):
    m32 = np.asarray(matrix, np.float32)
    hi = m32.astype(jnp.bfloat16)
    lo = (m32 - hi.astype(np.float32)).astype(jnp.bfloat16)
    return np.stack([hi, lo])


def dft_table():
    t = np.arange(N)
    f = np.arange(BINS)
    phases = ((t[:, None] * f[None, :]) % N).astype(np.float64) * (2.0 * math.pi / N)
    table = np.concatenate([np.cos(phases), -np.sin(phases)], 1)
    return table.astype(np.float32).astype(jnp.bfloat16)


def split(x):
    hi = x.astype(jnp.bfloat16)
    lo = (x - hi.astype(jnp.float32)).astype(jnp.bfloat16)
    return hi, lo


def dot(a, b, trans_b):
    dims = (((1,), (1 if trans_b else 0,)), ((), ()))
    return lax.dot_general(a, b, dims, preferred_element_type=jnp.float32)


def dot3(a, b, trans_b=False):
    return dot(a[0], b[0], trans_b) + (dot(a[1], b[0], trans_b) + dot(a[0], b[1], trans_b))


def greet_all():
    n_tm = lax.axis_size("tm")
    n = lax.axis_size("chan") * n_tm
    me = lax.axis_index("chan") * n_tm + lax.axis_index("tm")
    barrier = pltpu.get_barrier_semaphore()

    def greet(k, carry):
        d = lax.rem(me + k, n)
        pl.semaphore_signal(
            barrier, inc=1, device_id=(d // n_tm, lax.rem(d, n_tm)), device_id_type=MESH
        )
        return carry

    lax.fori_loop(1, n, greet, 0)
    pl.semaphore_wait(barrier, n - 1)


def gather_kernel(samples, slab, blocks, edge, send, recv, edge_send, edge_recv, own):
    n_chan, n_tm = lax.axis_size("chan"), lax.axis_size("tm")
    c, t = lax.axis_index("chan"), lax.axis_index("tm")
    rows, width = samples.shape
    count = width // BLOCK
    rep = n_chan // count
    values = samples[...]
    first = jnp.concatenate([values[:, width - HALF :], values[:, :HALF]], 1)
    blocks[0] = first
    blocks[count] = first
    for j in range(1, count):
        blocks[j] = values[:, BLOCK * j - HALF : BLOCK * j + HALF]
    greet_all()
    mine = pl.ds(pl.multiple_of(c * rows, rows), rows)
    place = c // rep

    def remote(to):
        return pltpu.make_async_remote_copy(
            src_ref=blocks.at[pl.ds(to // rep, 2)],
            dst_ref=slab.at[:, mine, :],
            send_sem=send.at[to],
            recv_sem=recv.at[c],
            device_id=(to, t),
            device_id_type=MESH,
        )

    def incoming(source):
        return pltpu.make_async_remote_copy(
            src_ref=blocks.at[pl.ds(0, 2)],
            dst_ref=slab.at[:, pl.ds(pl.multiple_of(source * rows, rows), rows), :],
            send_sem=send.at[source],
            recv_sem=recv.at[source],
            device_id=(source, t),
            device_id_type=MESH,
        )

    def rim(to, shift, r):
        return pltpu.make_async_remote_copy(
            src_ref=blocks.at[0],
            dst_ref=edge.at[mine, :],
            send_sem=edge_send.at[r],
            recv_sem=edge_recv.at[c],
            device_id=(to, lax.rem(t + shift, n_tm)),
            device_id_type=MESH,
        )

    for r in range(rep):
        rim(r, 1, r).start()
        rim((count - 1) * rep + r, n_tm - 1, rep + r).start()
    local = pltpu.make_async_copy(blocks.at[pl.ds(place, 2)], slab.at[:, mine, :], own)
    local.start()

    def start(k, carry):
        remote(lax.rem(c + k, n_chan)).start()
        return carry

    lax.fori_loop(1, n_chan, start, 0)
    local.wait()

    def finish(k, carry):
        incoming(lax.rem(c + n_chan - k, n_chan)).wait_recv()
        return carry

    lax.fori_loop(1, n_chan, finish, 0)
    at_edge = jnp.logical_or(place == 0, place == count - 1)

    @pl.when(at_edge)
    def _():
        def take(source, carry):
            pltpu.make_async_remote_copy(
                src_ref=blocks.at[0],
                dst_ref=edge.at[pl.ds(pl.multiple_of(source * rows, rows), rows), :],
                send_sem=edge_send.at[0],
                recv_sem=edge_recv.at[source],
                device_id=(source, lax.rem(t + 1, n_tm)),
                device_id_type=MESH,
            ).wait_recv()
            return carry

        lax.fori_loop(0, n_chan, take, 0)

    left = lax.broadcasted_iota(jnp.int32, edge.shape, 1) < HALF

    @pl.when(place == 0)
    def _():
        slab[0] = jnp.where(left, edge[...], slab[0])

    @pl.when(place == count - 1)
    def _():
        slab[1] = jnp.where(left, slab[1], edge[...])

    def sent(k, carry):
        remote(lax.rem(c + k, n_chan)).wait_send()
        return carry

    lax.fori_loop(1, n_chan, sent, 0)
    for r in range(rep):
        rim(r, 1, r).wait_send()
        rim((count - 1) * rep + r, n_tm - 1, rep + r).wait_send()


def shrink(aa, ab, ba, bb, cut_one, cut_two):
    root_half = 1.0 / math.sqrt(2.0)
    re1 = (aa - bb) * root_half
    im1 = (ab + ba) * root_half
    re2 = (aa + bb) * root_half
    im2 = (ab - ba) * root_half
    f1 = jnp.maximum(1.0 - cut_one * lax.rsqrt(re1 * re1 + im1 * im1), 0.0) * root_half
    f2 = jnp.maximum(1.0 - cut_two * lax.rsqrt(re2 * re2 + im2 * im2), 0.0) * root_half
    re1, im1, re2, im2 = re1 * f1, im1 * f1, re2 * f2, im2 * f2
    return re1 + re2, im1 + im2, im1 - im2, re2 - re1


def cut_maps(cuts, level, shape, low_rows, low_cols):
    row_low = lax.broadcasted_iota(jnp.int32, shape, 0) < low_rows
    col_low = lax.broadcasted_iota(jnp.int32, shape, 1) < low_cols
    pick = []
    for k in range(2):
        lh, hl, hh = (cuts[level, 2 * o + k].astype(jnp.float32) / 32.0 for o in range(3))
        pick.append(jnp.where(row_low, lh, jnp.where(col_low, hl, hh)))
    return pick[0], pick[1], jnp.logical_and(row_low, col_low)


def denoise_kernel(
    cuts, slab, sources, c1, c1t, t1, t1c, c2, c2t, t2, t2t, c3, c3t, t3, t3t,
    picked, cleaned, coefs,
):
    trees = [(0, 0), (0, 1), (1, 0), (1, 1)]
    rows = slab.shape[1]
    cols = 2 * BLOCK
    x = split(jnp.concatenate([slab[0], slab[1]], 1))
    first = split(dot3(x, (t1[0], t1[1]), True))
    coefs[...] = dot3((c1[0], c1[1]), first)
    hr, hc = rows // 2, cols // 2
    lows = []
    for p, q in trees:
        band = split(coefs[p * rows : p * rows + hr, q * cols : q * cols + hc])
        timed = split(dot3(band, (t2[0, q], t2[1, q]), True))
        lows.append(dot3((c2[0, p], c2[1, p]), timed))
    deep = []
    for tree, (p, q) in enumerate(trees):
        timed = split(dot3(split(lows[tree]), (t3[0, q], t3[1, q]), True))
        deep.append(dot3((c3[0, p], c3[1, p]), timed))
    one, two, kept = cut_maps(cuts, 2, deep[0].shape, hr // 4, hc // 4)
    shrunk = shrink(*deep, one, two)
    deep = [jnp.where(kept, a, b) for a, b in zip(deep, shrunk)]
    one, two, kept = cut_maps(cuts, 1, lows[0].shape, hr // 2, hc // 2)
    shrunk = shrink(*lows, one, two)
    for orient, (row_high, col_high) in enumerate([(0, 1), (1, 0), (1, 1)]):
        spots = [
            (
                slice(p * rows + row_high * hr, p * rows + row_high * hr + hr),
                slice(q * cols + col_high * hc, q * cols + col_high * hc + hc),
            )
            for p, q in trees
        ]
        top = [
            cuts[0, 2 * orient + k].astype(jnp.float32) / 32.0 for k in range(2)
        ]
        done = shrink(*[coefs[a, b] for a, b in spots], top[0], top[1])
        for (a, b), cell in zip(spots, done):
            coefs[a, b] = cell
    for tree, (p, q) in enumerate(trees):
        timed = split(dot3(split(deep[tree]), (t3t[0, q], t3t[1, q]), True))
        inner = dot3((c3t[0, p], c3t[1, p]), timed)
        band = jnp.where(kept, inner, shrunk[tree])
        timed = split(dot3(split(band), (t2t[0, q], t2t[1, q]), True))
        coefs[p * rows : p * rows + hr, q * cols : q * cols + hc] = dot3(
            (c2t[0, p], c2t[1, p]), timed
        )
    timed = split(dot3(split(coefs[...]), (t1c[0], t1c[1])))
    result = (0.25 * dot3((c1t[0], c1t[1]), timed)).astype(jnp.bfloat16)
    cleaned[...] = result.astype(jnp.float32)
    one_hot = jnp.where(
        lax.broadcasted_iota(jnp.int32, (sources.shape[0], rows), 1) == sources[...], 1.0, 0.0
    ).astype(jnp.bfloat16)
    picked[...] = dot(one_hot, result, False).astype(jnp.bfloat16)


def spread_kernel(picked, cleaned, picks, receivers, send, recv, send2, recv2, own):
    n_chan, n_tm = lax.axis_size("chan"), lax.axis_size("tm")
    c, t = lax.axis_index("chan"), lax.axis_index("tm")
    per_window = N // BLOCK
    blocks = picks.shape[0] * per_window
    count = blocks // n_tm
    rep = n_chan // count
    share = cleaned.shape[0] // (n_chan * n_tm)
    greet_all()

    def spot(block):
        return block // per_window, pl.ds(
            pl.multiple_of(lax.rem(block, per_window) * BLOCK, BLOCK), BLOCK
        )

    def rows_of(dc, dt):
        return pl.ds(pl.multiple_of((dc * n_tm + dt) * share // 8 * 8, 8), 8)

    w, cols = spot(t * count + c // rep)
    first = pltpu.make_async_copy(picked, picks.at[w, :, cols], own.at[0])
    second = pltpu.make_async_copy(
        cleaned.at[rows_of(c, t), :], receivers.at[w, :, cols], own.at[1]
    )

    def pair(k):
        dc = lax.rem(c // rep + k // n_tm, count) * rep + lax.rem(c, rep)
        dt = lax.rem(t + lax.rem(k, n_tm), n_tm)
        block = t * count + c // rep
        return (
            pltpu.make_async_remote_copy(
                src_ref=picked,
                dst_ref=picks.at[w, :, cols],
                send_sem=send.at[k],
                recv_sem=recv.at[block],
                device_id=(dc, dt),
                device_id_type=MESH,
            ),
            pltpu.make_async_remote_copy(
                src_ref=cleaned.at[rows_of(dc, dt), :],
                dst_ref=receivers.at[w, :, cols],
                send_sem=send2.at[k],
                recv_sem=recv2.at[block],
                device_id=(dc, dt),
                device_id_type=MESH,
            ),
        )

    def start(k, carry):
        for copy in pair(k):
            copy.start()
        return carry

    lax.fori_loop(1, blocks, start, 0)
    first.start()
    second.start()
    first.wait()
    second.wait()

    def finish(k, carry):
        block = lax.rem(t * count + c // rep + k, blocks)
        bw, bcols = spot(block)
        away = (lax.rem(block, count) * rep, block // count)
        pltpu.make_async_remote_copy(
            src_ref=picked,
            dst_ref=picks.at[bw, :, bcols],
            send_sem=send.at[0],
            recv_sem=recv.at[block],
            device_id=away,
            device_id_type=MESH,
        ).wait_recv()
        pltpu.make_async_remote_copy(
            src_ref=cleaned.at[pl.ds(0, 8), :],
            dst_ref=receivers.at[bw, :, bcols],
            send_sem=send2.at[0],
            recv_sem=recv2.at[block],
            device_id=away,
            device_id_type=MESH,
        ).wait_recv()
        return carry

    lax.fori_loop(1, blocks, finish, 0)

    def sent(k, carry):
        for copy in pair(k):
            copy.wait_send()
        return carry

    lax.fori_loop(1, blocks, sent, 0)


def correlate_kernel(picks, receivers, table, out, white, heard, cross):
    windows, sources = picks.shape[0], picks.shape[1]

    def whiten(block):
        spectra = dot(block, table[...], False)
        scale = lax.rsqrt(jnp.mean(spectra * spectra, axis=1, keepdims=True) + 1e-05)
        return (spectra * scale).astype(jnp.bfloat16).astype(jnp.float32)

    joined = jnp.concatenate(
        [picks[...].reshape(windows * sources, N)]
        + [receivers[...].reshape(windows * 8, N).astype(jnp.bfloat16)],
        0,
    )
    spectra = whiten(joined)
    base = windows * sources
    for part in range(N // BLOCK):
        white[part] = spectra[:base, BLOCK * part : BLOCK * (part + 1)]
    for w in range(windows):
        heard[w] = spectra[base + 8 * w : base + 8 * w + 8]
    weight = jnp.where(lax.broadcasted_iota(jnp.int32, (1, BLOCK), 1) == 0, 1.0, 2.0)

    def body(g, carry):
        for chunk in range(BINS // BLOCK):
            lo = chunk * BLOCK
            hi = BINS + lo
            real = [None, None]
            imag = [None, None]
            for w in range(windows):
                rr = heard[w, :, lo : lo + BLOCK]
                ri = heard[w, :, hi : hi + BLOCK]
                for j in range(2):
                    spread = pl.ds(w * sources + 2 * g + j, 8, stride=0)
                    pr = white.at[chunk][spread, :]
                    pi = white.at[chunk + BINS // BLOCK][spread, :]
                    a = pr * rr + pi * ri
                    b = pi * rr - pr * ri
                    real[j] = a if real[j] is None else real[j] + a
                    imag[j] = b if imag[j] is None else imag[j] + b
            factor = weight if chunk == 0 else 2.0
            spot = pl.ds(pl.multiple_of(16 * g, 16), 16)
            cross[spot, lo : lo + BLOCK] = (jnp.concatenate(real, 0) * factor).astype(jnp.bfloat16)
            cross[spot, hi : hi + BLOCK] = (jnp.concatenate(imag, 0) * factor).astype(jnp.bfloat16)
        return carry

    lax.fori_loop(0, sources // 2, body, 0)
    scale = 1.0 / math.sqrt(windows * N)
    half = LAGS // 2
    lags = jnp.concatenate([table[N - half :, :], table[:half, :]], 0)
    out[...] = dot(cross[...], lags, True) * scale


def local(samples, thresholds, sources):
    n_chan, n_tm = lax.axis_size("chan"), lax.axis_size("tm")
    rows, width = samples.shape
    channels = rows * n_chan
    count = width // BLOCK
    rep = n_chan // count
    blocks = count * n_tm
    windows = n_tm * width // N
    picked_count = sources.shape[0]
    vmem = pl.BlockSpec(memory_space=pltpu.VMEM)
    smem = pl.BlockSpec(memory_space=pltpu.SMEM)
    dma = pltpu.SemaphoreType.DMA
    f32, bf16 = jnp.float32, jnp.bfloat16
    big = 60 * 1024 * 1024

    slab = pl.pallas_call(
        gather_kernel,
        out_shape=jax.ShapeDtypeStruct((2, channels, BLOCK), f32),
        in_specs=[vmem],
        out_specs=vmem,
        scratch_shapes=[
            pltpu.VMEM((count + 1, rows, BLOCK), f32),
            pltpu.VMEM((channels, BLOCK), f32),
            dma((n_chan,)),
            dma((n_chan,)),
            dma((2 * rep,)),
            dma((n_chan,)),
            dma,
        ],
        compiler_params=pltpu.CompilerParams(collective_id=0, has_side_effects=True),
        name="gather_slab",
    )(samples)

    def wide(matrix):
        return halves(matrix.reshape(-1, matrix.shape[-1]))

    def flipped(matrix):
        return np.swapaxes(matrix, -1, -2)

    def padded_low(matrix):
        return np.concatenate([matrix, np.zeros_like(matrix)], -1)

    chan = [bank_matrix(channels >> j) for j in range(3)]
    time = [bank_matrix(2 * BLOCK >> j) for j in range(3)]
    c1, t1 = wide(chan[0]), wide(time[0])
    c3, t3 = padded_low(chan[2]), padded_low(time[2])
    tables = [
        c1,
        np.ascontiguousarray(flipped(c1)),
        t1,
        np.ascontiguousarray(t1[:, :, HALF : HALF + BLOCK]),
        halves(chan[1]),
        halves(flipped(chan[1])),
        halves(time[1]),
        halves(flipped(time[1])),
        halves(c3),
        halves(flipped(c3)),
        halves(t3),
        halves(flipped(t3)),
    ]
    picked, cleaned = pl.pallas_call(
        denoise_kernel,
        out_shape=(
            jax.ShapeDtypeStruct((picked_count, BLOCK), bf16),
            jax.ShapeDtypeStruct((channels, BLOCK), f32),
        ),
        in_specs=[smem] + [vmem] * (2 + len(tables)),
        out_specs=(vmem, vmem),
        scratch_shapes=[pltpu.VMEM((2 * channels, 4 * BLOCK), f32)],
        compiler_params=pltpu.CompilerParams(vmem_limit_bytes=big),
        name="denoise",
    )(thresholds, slab, sources[:, None], *[jnp.asarray(a) for a in tables])

    picks, receivers = pl.pallas_call(
        spread_kernel,
        out_shape=(
            jax.ShapeDtypeStruct((windows, picked_count, N), bf16),
            jax.ShapeDtypeStruct((windows, 8, N), f32),
        ),
        in_specs=[vmem, vmem],
        out_specs=(vmem, vmem),
        scratch_shapes=[dma((blocks,)), dma((blocks,)), dma((blocks,)), dma((blocks,)), dma((2,))],
        compiler_params=pltpu.CompilerParams(collective_id=1, has_side_effects=True),
        name="spread",
    )(picked, cleaned)

    out = pl.pallas_call(
        correlate_kernel,
        out_shape=jax.ShapeDtypeStruct((picked_count * 8, LAGS), f32),
        in_specs=[vmem] * 3,
        out_specs=vmem,
        scratch_shapes=[
            pltpu.VMEM((N // BLOCK, windows * picked_count, BLOCK), f32),
            pltpu.VMEM((windows, 8, N), f32),
            pltpu.VMEM((picked_count * 8, N), bf16),
        ],
        compiler_params=pltpu.CompilerParams(vmem_limit_bytes=big),
        name="correlate",
    )(picks, receivers, jnp.asarray(dft_table()))
    out = out.reshape(picked_count, 8, LAGS)
    share = channels // (n_chan * n_tm)
    if share < 8:
        place = lax.axis_index("chan") * n_tm + lax.axis_index("tm")
        out = lax.dynamic_slice_in_dim(out, lax.rem(place * share, 8), share, 1)
    return out


def solution(mesh):
    return jax.shard_map(
        local,
        mesh=mesh,
        in_specs=(P("chan", "tm"), P(), P()),
        out_specs=P(None, ("chan", "tm"), None),
        check_vma=False,
    )
```

```python
import functools
import math

import jax
import jax.numpy as jnp
import numpy as np
from jax import lax
from jax.experimental import pallas as pl
from jax.experimental.pallas import tpu as pltpu
from jax.sharding import PartitionSpec as P

N = 1024
LEVELS = 3
BINS = 512
LAGS = 512
BLOCK = 128
HALF = 64
MESH = pl.DeviceIdType.MESH

daubechies = [
    0.2303778133088964,
    0.7148465705529155,
    0.6308807679298587,
    -0.0279837694168599,
    -0.1870348117190931,
    0.0308413818355607,
    0.0328830116668852,
    -0.010597401785069,
]


def filter_bank():
    lowpass = list(daubechies)
    highpass = [(1.0 if k % 2 == 0 else -1.0) * daubechies[7 - k] for k in range(8)]
    return [(lowpass, highpass), (lowpass[::-1], highpass[::-1])]


def bank_matrix(length):
    half = length // 2
    out = np.zeros((2, 2, half, length))
    rows = np.arange(half)
    for tree, pair in enumerate(filter_bank()):
        for band, taps in enumerate(pair):
            for k in range(8):
                np.add.at(out[tree, band], (rows, (2 * rows + k - 3) % length), taps[k])
    return out.reshape(2, length, length)


def halves(matrix):
    m32 = np.asarray(matrix, np.float32)
    hi = m32.astype(jnp.bfloat16)
    lo = (m32 - hi.astype(np.float32)).astype(jnp.bfloat16)
    return np.stack([hi, lo])


def dft_table():
    t = np.arange(N)
    f = np.arange(BINS)
    phases = ((t[:, None] * f[None, :]) % N).astype(np.float64) * (2.0 * math.pi / N)
    table = np.concatenate([np.cos(phases), -np.sin(phases)], 1)
    return table.astype(np.float32).astype(jnp.bfloat16)


def split(x):
    hi = x.astype(jnp.bfloat16)
    lo = (x - hi.astype(jnp.float32)).astype(jnp.bfloat16)
    return hi, lo


def dot(a, b, trans_b):
    dims = (((1,), (1 if trans_b else 0,)), ((), ()))
    return lax.dot_general(a, b, dims, preferred_element_type=jnp.float32)


def dot3(a, b, trans_b=False):
    return dot(a[0], b[0], trans_b) + (dot(a[1], b[0], trans_b) + dot(a[0], b[1], trans_b))


def greet_all():
    n_tm = lax.axis_size("tm")
    n = lax.axis_size("chan") * n_tm
    me = lax.axis_index("chan") * n_tm + lax.axis_index("tm")
    barrier = pltpu.get_barrier_semaphore()

    def greet(k, carry):
        d = lax.rem(me + k, n)
        pl.semaphore_signal(
            barrier, inc=1, device_id=(d // n_tm, lax.rem(d, n_tm)), device_id_type=MESH
        )
        return carry

    lax.fori_loop(1, n, greet, 0)
    pl.semaphore_wait(barrier, n - 1)


def gather(samples, slab, blocks, edge, send, recv, edge_send, edge_recv, own):
    n_chan, n_tm = lax.axis_size("chan"), lax.axis_size("tm")
    c, t = lax.axis_index("chan"), lax.axis_index("tm")
    rows, width = samples.shape
    count = width // BLOCK
    rep = n_chan // count
    values = samples[...]
    for j in range(count):
        right, left = (BLOCK * (j + 1)) % width, (BLOCK * j - HALF) % width
        blocks[2 * j] = values[:, BLOCK * j : BLOCK * (j + 1)]
        blocks[2 * j + 1] = jnp.concatenate(
            [values[:, right : right + HALF], values[:, left : left + HALF]], 1
        )
    blocks[2 * count] = jnp.concatenate([values[:, :HALF], values[:, width - HALF :]], 1)
    greet_all()
    mine = pl.ds(pl.multiple_of(c * rows, rows), rows)
    place = c // rep

    def remote(to):
        return pltpu.make_async_remote_copy(
            src_ref=blocks.at[pl.ds(to // rep * 2, 2)],
            dst_ref=slab.at[:, mine, :],
            send_sem=send.at[to],
            recv_sem=recv.at[c],
            device_id=(to, t),
            device_id_type=MESH,
        )

    def incoming(source):
        return pltpu.make_async_remote_copy(
            src_ref=blocks.at[pl.ds(0, 2)],
            dst_ref=slab.at[:, pl.ds(pl.multiple_of(source * rows, rows), rows), :],
            send_sem=send.at[source],
            recv_sem=recv.at[source],
            device_id=(source, t),
            device_id_type=MESH,
        )

    def rim(to, shift, r):
        return pltpu.make_async_remote_copy(
            src_ref=blocks.at[2 * count],
            dst_ref=edge.at[mine, :],
            send_sem=edge_send.at[r],
            recv_sem=edge_recv.at[c],
            device_id=(to, lax.rem(t + shift, n_tm)),
            device_id_type=MESH,
        )

    for r in range(rep):
        rim(r, 1, r).start()
        rim((count - 1) * rep + r, n_tm - 1, rep + r).start()
    local = pltpu.make_async_copy(blocks.at[pl.ds(place * 2, 2)], slab.at[:, mine, :], own)
    local.start()

    def start(k, carry):
        remote(lax.rem(c + k, n_chan)).start()
        return carry

    lax.fori_loop(1, n_chan, start, 0)
    local.wait()

    def finish(k, carry):
        incoming(lax.rem(c + n_chan - k, n_chan)).wait_recv()
        return carry

    lax.fori_loop(1, n_chan, finish, 0)
    at_edge = jnp.logical_or(place == 0, place == count - 1)

    @pl.when(at_edge)
    def _():
        def take(source, carry):
            pltpu.make_async_remote_copy(
                src_ref=blocks.at[2 * count],
                dst_ref=edge.at[pl.ds(pl.multiple_of(source * rows, rows), rows), :],
                send_sem=edge_send.at[0],
                recv_sem=edge_recv.at[source],
                device_id=(source, lax.rem(t + 1, n_tm)),
                device_id_type=MESH,
            ).wait_recv()
            return carry

        lax.fori_loop(0, n_chan, take, 0)

    left = lax.broadcasted_iota(jnp.int32, edge.shape, 1) < HALF

    @pl.when(place == 0)
    def _():
        slab[1] = jnp.where(left, slab[1], edge[...])

    @pl.when(place == count - 1)
    def _():
        slab[1] = jnp.where(left, edge[...], slab[1])

    def sent(k, carry):
        remote(lax.rem(c + k, n_chan)).wait_send()
        return carry

    lax.fori_loop(1, n_chan, sent, 0)
    for r in range(rep):
        rim(r, 1, r).wait_send()
        rim((count - 1) * rep + r, n_tm - 1, rep + r).wait_send()


def shrink(aa, ab, ba, bb, cut_one, cut_two):
    root_half = 1.0 / math.sqrt(2.0)
    re1 = (aa - bb) * root_half
    im1 = (ab + ba) * root_half
    re2 = (aa + bb) * root_half
    im2 = (ab - ba) * root_half
    f1 = jnp.maximum(1.0 - cut_one * lax.rsqrt(re1 * re1 + im1 * im1), 0.0) * root_half
    f2 = jnp.maximum(1.0 - cut_two * lax.rsqrt(re2 * re2 + im2 * im2), 0.0) * root_half
    re1, im1, re2, im2 = re1 * f1, im1 * f1, re2 * f2, im2 * f2
    return re1 + re2, im1 + im2, im1 - im2, re2 - re1


def cut_maps(cuts, level, shape, low_rows, low_cols):
    row_low = lax.broadcasted_iota(jnp.int32, shape, 0) < low_rows
    col_low = lax.broadcasted_iota(jnp.int32, shape, 1) < low_cols
    pick = []
    for k in range(2):
        lh, hl, hh = (cuts[level, 2 * o + k].astype(jnp.float32) / 32.0 for o in range(3))
        pick.append(jnp.where(row_low, lh, jnp.where(col_low, hl, hh)))
    return pick[0], pick[1], jnp.logical_and(row_low, col_low)


def denoise(cuts, slab, sources, tables, picked, cleaned, coefs):
    c1, c1t, t1, c2, c2t, t2, t2t, c3, c3t, t3, t3t = tables
    trees = [(0, 0), (0, 1), (1, 0), (1, 1)]
    rows = slab.shape[1]
    cols = 2 * BLOCK
    x = split(jnp.concatenate([slab[0], slab[1]], 1))
    first = split(dot3(x, (t1[0], t1[1]), True))
    coefs[...] = dot3((c1[0], c1[1]), first)
    hr, hc = rows // 2, cols // 2
    lows = []
    for p, q in trees:
        band = split(coefs[p * rows : p * rows + hr, q * cols : q * cols + hc])
        timed = split(dot3(band, (t2[0, q], t2[1, q]), True))
        lows.append(dot3((c2[0, p], c2[1, p]), timed))
    deep = []
    for tree, (p, q) in enumerate(trees):
        timed = split(dot3(split(lows[tree]), (t3[0, q], t3[1, q]), True))
        deep.append(dot3((c3[0, p], c3[1, p]), timed))
    one, two, kept = cut_maps(cuts, 2, deep[0].shape, hr // 4, hc // 4)
    shrunk = shrink(*deep, one, two)
    deep = [jnp.where(kept, a, b) for a, b in zip(deep, shrunk)]
    one, two, kept = cut_maps(cuts, 1, lows[0].shape, hr // 2, hc // 2)
    shrunk = shrink(*lows, one, two)
    for orient, (row_high, col_high) in enumerate([(0, 1), (1, 0), (1, 1)]):
        spots = [
            (
                slice(p * rows + row_high * hr, p * rows + row_high * hr + hr),
                slice(q * cols + col_high * hc, q * cols + col_high * hc + hc),
            )
            for p, q in trees
        ]
        top = [
            cuts[0, 2 * orient + k].astype(jnp.float32) / 32.0 for k in range(2)
        ]
        done = shrink(*[coefs[a, b] for a, b in spots], top[0], top[1])
        for (a, b), cell in zip(spots, done):
            coefs[a, b] = cell
    for tree, (p, q) in enumerate(trees):
        timed = split(dot3(split(deep[tree]), (t3t[0, q], t3t[1, q]), True))
        inner = dot3((c3t[0, p], c3t[1, p]), timed)
        band = jnp.where(kept, inner, shrunk[tree])
        timed = split(dot3(split(band), (t2t[0, q], t2t[1, q]), True))
        coefs[p * rows : p * rows + hr, q * cols : q * cols + hc] = dot3(
            (c2t[0, p], c2t[1, p]), timed
        )
    timed = split(dot3(split(coefs[...]), (t1[0, :, :BLOCK], t1[1, :, :BLOCK])))
    result = (0.25 * dot3((c1t[0], c1t[1]), timed)).astype(jnp.bfloat16)
    cleaned[...] = result.astype(jnp.float32).reshape(rows // 8, 8, BLOCK).astype(jnp.bfloat16)
    one_hot = jnp.where(
        lax.broadcasted_iota(jnp.int32, (rows, sources.shape[1]), 0) == sources[...], 1.0, 0.0
    )
    chosen = jnp.transpose(one_hot).astype(jnp.bfloat16)
    picked[...] = dot(chosen, result, False).astype(jnp.bfloat16)


def spread(picks, cleaned, receivers, near, far, across, recv, send, land, own):
    n_chan, n_tm = lax.axis_size("chan"), lax.axis_size("tm")
    c, t = lax.axis_index("chan"), lax.axis_index("tm")
    blocks = picks.shape[0]
    count = blocks // n_tm
    rep = n_chan // count
    pairs = n_tm // 2
    share = cleaned.shape[0] * 8 // (n_chan * n_tm)
    place, copy_index, core = c // rep, lax.rem(c, rep), lax.rem(t, 2)
    mine = t * count + place

    def move(block, sem, chan, tm):
        return pltpu.make_async_remote_copy(
            src_ref=picks.at[block],
            dst_ref=picks.at[block],
            send_sem=sem,
            recv_sem=recv.at[block],
            device_id=(chan, tm),
            device_id_type=MESH,
        )

    def group(k):
        return move(mine, near.at[k], lax.rem(place + k, count) * rep + copy_index, t)

    def along(u, k):
        block = t * count + lax.rem(place + count - k, count)
        to = lax.rem(t // 2 + u, pairs) * 2 + core
        return move(block, far.at[u * count + k], c, to)

    def beside(u, k):
        other = lax.rem(t // 2 + pairs - u, pairs) * 2 + core
        block = other * count + lax.rem(place + count - k, count)
        return move(block, across.at[u * count + k], c, t + 1 - 2 * core)

    def rows_of(dc, dt):
        return (dc * n_tm + dt) * share // 8

    def personal(k):
        dc = lax.rem(place + k // n_tm, count) * rep + copy_index
        dt = lax.rem(t + lax.rem(k, n_tm), n_tm)
        return pltpu.make_async_remote_copy(
            src_ref=cleaned.at[rows_of(dc, dt)],
            dst_ref=receivers.at[mine],
            send_sem=send.at[k],
            recv_sem=land.at[mine],
            device_id=(dc, dt),
            device_id_type=MESH,
        )

    def each(low, high, act):
        def body(k, carry):
            act(k)
            return carry

        lax.fori_loop(low, high, body, 0)

    def await_block(block):
        move(block, near.at[0], c, t + 1 - 2 * core).wait_recv()

    def relay(k):
        @pl.when(k > 0)
        def _():
            await_block(t * count + lax.rem(place + count - k, count))

        for u in range(1, pairs):
            along(u, k).start()
        beside(0, k).start()

    each(1, count, lambda k: group(k).start())
    local = pltpu.make_async_copy(cleaned.at[rows_of(c, t)], receivers.at[mine], own)
    local.start()
    relay(0)
    each(1, blocks, lambda k: personal(k).start())
    each(1, count, relay)
    for u in range(1, pairs):

        def cross_over(k, u=u):
            other = lax.rem(t // 2 + pairs - u, pairs) * 2 + core
            await_block(other * count + lax.rem(place + count - k, count))
            beside(u, k).start()

        each(0, count, cross_over)
    for u in range(pairs):

        def last(k, u=u):
            other = lax.rem(t // 2 + pairs - u, pairs) * 2 + 1 - core
            await_block(other * count + lax.rem(place + count - k, count))

        each(0, count, last)

    def landed(k):
        block = lax.rem(mine + k, blocks)
        pltpu.make_async_remote_copy(
            src_ref=cleaned.at[0],
            dst_ref=receivers.at[block],
            send_sem=send.at[0],
            recv_sem=land.at[block],
            device_id=(c, t + 1 - 2 * core),
            device_id_type=MESH,
        ).wait_recv()

    local.wait()
    each(1, blocks, landed)
    each(1, count, lambda k: group(k).wait_send())
    each(1, blocks, lambda k: personal(k).wait_send())
    for u in range(pairs):
        each(0, count, lambda k, u=u: beside(u, k).wait_send())
        if u:
            each(0, count, lambda k, u=u: along(u, k).wait_send())


def clean_kernel(n_tables, same, cuts, samples, sources, *refs):
    stored, refs = refs[:n_tables], refs[n_tables:]
    picks, receivers = refs[:2]
    held, refs = refs[2 : 2 + n_tables], refs[2 + n_tables :]
    slab, blocks, edge, coefs, cleaned, loads = refs[:6]
    gather_sems, spread_sems = refs[6:11], refs[11:]
    copies = [pltpu.make_async_copy(a, b, loads.at[i]) for i, (a, b) in enumerate(zip(stored, held))]
    for copy in copies:
        copy.start()
    gather(samples, slab, blocks, edge, *gather_sems)
    for copy in copies:
        copy.wait()
    tables = [held[1], *held] if same else list(held)
    n_tm = lax.axis_size("tm")
    count = picks.shape[0] // n_tm
    rep = lax.axis_size("chan") // count
    mine = lax.axis_index("tm") * count + lax.axis_index("chan") // rep
    denoise(cuts, slab, sources, tables, picks.at[mine], cleaned, coefs)
    spread(picks, cleaned, receivers, *spread_sems)


def correlate_kernel(picks, receivers, table, out, white, heard, cross):
    per_window = N // BLOCK
    windows, sources = picks.shape[0] // per_window, picks.shape[1]

    def window(ref, w):
        return jnp.concatenate([ref[w * per_window + j] for j in range(per_window)], 1)

    def whiten(block):
        spectra = dot(block, table[...], False)
        scale = lax.rsqrt(jnp.mean(spectra * spectra, axis=1, keepdims=True) + 1e-05)
        return (spectra * scale).astype(jnp.bfloat16).astype(jnp.float32)

    heard_rows = [window(receivers, w).astype(jnp.float32) for w in range(windows)]
    joined = jnp.concatenate(
        [window(picks, w) for w in range(windows)]
        + [jnp.concatenate(heard_rows, 0).astype(jnp.bfloat16)],
        0,
    )
    spectra = whiten(joined)
    base = windows * sources
    for part in range(N // BLOCK):
        white[part] = spectra[:base, BLOCK * part : BLOCK * (part + 1)]
    for w in range(windows):
        heard[w] = spectra[base + 8 * w : base + 8 * w + 8]
    weight = jnp.where(lax.broadcasted_iota(jnp.int32, (1, BLOCK), 1) == 0, 1.0, 2.0)

    def body(g, carry):
        for chunk in range(BINS // BLOCK):
            lo = chunk * BLOCK
            hi = BINS + lo
            real = [None, None]
            imag = [None, None]
            for w in range(windows):
                rr = heard[w, :, lo : lo + BLOCK]
                ri = heard[w, :, hi : hi + BLOCK]
                for j in range(2):
                    spread = pl.ds(w * sources + 2 * g + j, 8, stride=0)
                    pr = white.at[chunk][spread, :]
                    pi = white.at[chunk + BINS // BLOCK][spread, :]
                    a = pr * rr + pi * ri
                    b = pi * rr - pr * ri
                    real[j] = a if real[j] is None else real[j] + a
                    imag[j] = b if imag[j] is None else imag[j] + b
            factor = weight if chunk == 0 else 2.0
            spot = pl.ds(pl.multiple_of(16 * g, 16), 16)
            cross[spot, lo : lo + BLOCK] = (jnp.concatenate(real, 0) * factor).astype(jnp.bfloat16)
            cross[spot, hi : hi + BLOCK] = (jnp.concatenate(imag, 0) * factor).astype(jnp.bfloat16)
        return carry

    lax.fori_loop(0, sources // 2, body, 0)
    scale = 1.0 / math.sqrt(windows * N)
    half = LAGS // 2
    lags = jnp.concatenate([table[N - half :, :], table[:half, :]], 0)
    out[...] = dot(cross[...], lags, True) * scale


def local(samples, thresholds, sources):
    n_chan, n_tm = lax.axis_size("chan"), lax.axis_size("tm")
    rows, width = samples.shape
    channels = rows * n_chan
    count = width // BLOCK
    rep = n_chan // count
    blocks = count * n_tm
    windows = n_tm * width // N
    picked_count = sources.shape[0]
    vmem = pl.BlockSpec(memory_space=pltpu.VMEM)
    smem = pl.BlockSpec(memory_space=pltpu.SMEM)
    dma = pltpu.SemaphoreType.DMA
    f32, bf16 = jnp.float32, jnp.bfloat16
    big = 60 * 1024 * 1024

    def wide(matrix):
        return halves(matrix.reshape(-1, matrix.shape[-1]))

    def flipped(matrix):
        return np.swapaxes(matrix, -1, -2)

    def padded_low(matrix):
        return np.concatenate([matrix, np.zeros_like(matrix)], -1)

    chan = [bank_matrix(channels >> j) for j in range(3)]
    time = [bank_matrix(2 * BLOCK >> j) for j in range(3)]
    c1, t1 = wide(chan[0]), wide(time[0])
    c3, t3 = padded_low(chan[2]), padded_low(time[2])
    same = channels == 2 * BLOCK
    tables = ([] if same else [c1]) + [
        np.ascontiguousarray(flipped(c1)),
        t1,
        halves(chan[1]),
        halves(flipped(chan[1])),
        halves(time[1]),
        halves(flipped(time[1])),
        halves(c3),
        halves(flipped(c3)),
        halves(t3),
        halves(flipped(t3)),
    ]
    far_count = blocks // 2
    picks, receivers = pl.pallas_call(
        functools.partial(clean_kernel, len(tables), same),
        out_shape=(
            jax.ShapeDtypeStruct((blocks, picked_count, BLOCK), bf16),
            jax.ShapeDtypeStruct((blocks, 8, BLOCK), bf16),
        ),
        in_specs=[smem, vmem, vmem] + [pl.BlockSpec(memory_space=pl.ANY)] * len(tables),
        out_specs=(vmem, vmem),
        scratch_shapes=[pltpu.VMEM(a.shape, bf16) for a in tables]
        + [
            pltpu.VMEM((2, channels, BLOCK), f32),
            pltpu.VMEM((2 * count + 1, rows, BLOCK), f32),
            pltpu.VMEM((channels, BLOCK), f32),
            pltpu.VMEM((2 * channels, 4 * BLOCK), f32),
            pltpu.VMEM((channels // 8, 8, BLOCK), bf16),
            dma((len(tables),)),
            dma((n_chan,)),
            dma((n_chan,)),
            dma((2 * rep,)),
            dma((n_chan,)),
            dma,
            dma((count,)),
            dma((far_count,)),
            dma((far_count,)),
            dma((blocks,)),
            dma((blocks,)),
            dma((blocks,)),
            dma,
        ],
        compiler_params=pltpu.CompilerParams(
            collective_id=0, has_side_effects=True, vmem_limit_bytes=big
        ),
        name="clean",
    )(thresholds, samples, sources[None, :], *[jnp.asarray(a) for a in tables])

    out = pl.pallas_call(
        correlate_kernel,
        out_shape=jax.ShapeDtypeStruct((picked_count * 8, LAGS), f32),
        in_specs=[vmem] * 3,
        out_specs=vmem,
        scratch_shapes=[
            pltpu.VMEM((N // BLOCK, windows * picked_count, BLOCK), f32),
            pltpu.VMEM((windows, 8, N), f32),
            pltpu.VMEM((picked_count * 8, N), bf16),
        ],
        compiler_params=pltpu.CompilerParams(vmem_limit_bytes=big),
        name="correlate",
    )(picks, receivers, jnp.asarray(dft_table()))
    out = out.reshape(picked_count, 8, LAGS)
    share = channels // (n_chan * n_tm)
    if share < 8:
        place = lax.axis_index("chan") * n_tm + lax.axis_index("tm")
        out = lax.dynamic_slice_in_dim(out, lax.rem(place * share, 8), share, 1)
    return out


def solution(mesh):
    return jax.shard_map(
        local,
        mesh=mesh,
        in_specs=(P("chan", "tm"), P(), P()),
        out_specs=P(None, ("chan", "tm"), None),
        check_vma=False,
    )
```

```python
import functools
import math

import jax
import jax.numpy as jnp
import numpy as np
from jax import lax
from jax.experimental import pallas as pl
from jax.experimental.pallas import tpu as pltpu
from jax.sharding import PartitionSpec as P

N = 1024
LEVELS = 3
BINS = 512
LAGS = 512
BLOCK = 128
HALF = 64
MESH = pl.DeviceIdType.MESH

daubechies = [
    0.2303778133088964,
    0.7148465705529155,
    0.6308807679298587,
    -0.0279837694168599,
    -0.1870348117190931,
    0.0308413818355607,
    0.0328830116668852,
    -0.010597401785069,
]


def filter_bank():
    lowpass = list(daubechies)
    highpass = [(1.0 if k % 2 == 0 else -1.0) * daubechies[7 - k] for k in range(8)]
    return [(lowpass, highpass), (lowpass[::-1], highpass[::-1])]


def bank_matrix(length):
    half = length // 2
    out = np.zeros((2, 2, half, length))
    rows = np.arange(half)
    for tree, pair in enumerate(filter_bank()):
        for band, taps in enumerate(pair):
            for k in range(8):
                np.add.at(out[tree, band], (rows, (2 * rows + k - 3) % length), taps[k])
    return out.reshape(2, length, length)


def halves(matrix):
    m32 = np.asarray(matrix, np.float32)
    hi = m32.astype(jnp.bfloat16)
    lo = (m32 - hi.astype(np.float32)).astype(jnp.bfloat16)
    return np.stack([hi, lo])


def dft_table():
    t = np.arange(N)
    f = np.arange(BINS)
    phases = ((t[:, None] * f[None, :]) % N).astype(np.float64) * (2.0 * math.pi / N)
    table = np.concatenate([np.cos(phases), -np.sin(phases)], 1)
    return table.astype(np.float32).astype(jnp.bfloat16)


def split(x):
    hi = x.astype(jnp.bfloat16)
    lo = (x - hi.astype(jnp.float32)).astype(jnp.bfloat16)
    return hi, lo


def dot(a, b, trans_b):
    dims = (((1,), (1 if trans_b else 0,)), ((), ()))
    return lax.dot_general(a, b, dims, preferred_element_type=jnp.float32)


def dot3(a, b, trans_b=False):
    return dot(a[0], b[0], trans_b) + (dot(a[1], b[0], trans_b) + dot(a[0], b[1], trans_b))


def greet_all():
    n_tm = lax.axis_size("tm")
    n = lax.axis_size("chan") * n_tm
    me = lax.axis_index("chan") * n_tm + lax.axis_index("tm")
    barrier = pltpu.get_barrier_semaphore()

    def greet(k, carry):
        d = lax.rem(me + k, n)
        pl.semaphore_signal(
            barrier, inc=1, device_id=(d // n_tm, lax.rem(d, n_tm)), device_id_type=MESH
        )
        return carry

    lax.fori_loop(1, n, greet, 0)
    pl.semaphore_wait(barrier, n - 1)


def gather(samples, slab, blocks, edge, send, recv, edge_send, edge_recv, own):
    n_chan, n_tm = lax.axis_size("chan"), lax.axis_size("tm")
    c, t = lax.axis_index("chan"), lax.axis_index("tm")
    rows, width = samples.shape
    count = width // BLOCK
    rep = n_chan // count
    values = samples[...]
    for j in range(count):
        right, left = (BLOCK * (j + 1)) % width, (BLOCK * j - HALF) % width
        blocks[2 * j] = values[:, BLOCK * j : BLOCK * (j + 1)]
        blocks[2 * j + 1] = jnp.concatenate(
            [values[:, right : right + HALF], values[:, left : left + HALF]], 1
        )
    blocks[2 * count] = jnp.concatenate([values[:, :HALF], values[:, width - HALF :]], 1)
    greet_all()
    mine = pl.ds(pl.multiple_of(c * rows, rows), rows)
    place = c // rep

    def remote(to):
        return pltpu.make_async_remote_copy(
            src_ref=blocks.at[pl.ds(to // rep * 2, 2)],
            dst_ref=slab.at[:, mine, :],
            send_sem=send.at[to],
            recv_sem=recv.at[c],
            device_id=(to, t),
            device_id_type=MESH,
        )

    def incoming(source):
        return pltpu.make_async_remote_copy(
            src_ref=blocks.at[pl.ds(0, 2)],
            dst_ref=slab.at[:, pl.ds(pl.multiple_of(source * rows, rows), rows), :],
            send_sem=send.at[source],
            recv_sem=recv.at[source],
            device_id=(source, t),
            device_id_type=MESH,
        )

    def rim(to, shift, r):
        return pltpu.make_async_remote_copy(
            src_ref=blocks.at[2 * count],
            dst_ref=edge.at[mine, :],
            send_sem=edge_send.at[r],
            recv_sem=edge_recv.at[c],
            device_id=(to, lax.rem(t + shift, n_tm)),
            device_id_type=MESH,
        )

    for r in range(rep):
        rim(r, 1, r).start()
        rim((count - 1) * rep + r, n_tm - 1, rep + r).start()
    local = pltpu.make_async_copy(blocks.at[pl.ds(place * 2, 2)], slab.at[:, mine, :], own)
    local.start()

    def start(k, carry):
        remote(lax.rem(c + k, n_chan)).start()
        return carry

    lax.fori_loop(1, n_chan, start, 0)
    local.wait()

    def finish(k, carry):
        incoming(lax.rem(c + n_chan - k, n_chan)).wait_recv()
        return carry

    lax.fori_loop(1, n_chan, finish, 0)
    at_edge = jnp.logical_or(place == 0, place == count - 1)

    @pl.when(at_edge)
    def _():
        def take(source, carry):
            pltpu.make_async_remote_copy(
                src_ref=blocks.at[2 * count],
                dst_ref=edge.at[pl.ds(pl.multiple_of(source * rows, rows), rows), :],
                send_sem=edge_send.at[0],
                recv_sem=edge_recv.at[source],
                device_id=(source, lax.rem(t + 1, n_tm)),
                device_id_type=MESH,
            ).wait_recv()
            return carry

        lax.fori_loop(0, n_chan, take, 0)

    left = lax.broadcasted_iota(jnp.int32, edge.shape, 1) < HALF

    @pl.when(place == 0)
    def _():
        slab[1] = jnp.where(left, slab[1], edge[...])

    @pl.when(place == count - 1)
    def _():
        slab[1] = jnp.where(left, edge[...], slab[1])

    def sent(k, carry):
        remote(lax.rem(c + k, n_chan)).wait_send()
        return carry

    lax.fori_loop(1, n_chan, sent, 0)
    for r in range(rep):
        rim(r, 1, r).wait_send()
        rim((count - 1) * rep + r, n_tm - 1, rep + r).wait_send()


def shrink(aa, ab, ba, bb, cut_one, cut_two):
    root_half = 1.0 / math.sqrt(2.0)
    re1 = (aa - bb) * root_half
    im1 = (ab + ba) * root_half
    re2 = (aa + bb) * root_half
    im2 = (ab - ba) * root_half
    f1 = jnp.maximum(1.0 - cut_one * lax.rsqrt(re1 * re1 + im1 * im1), 0.0) * root_half
    f2 = jnp.maximum(1.0 - cut_two * lax.rsqrt(re2 * re2 + im2 * im2), 0.0) * root_half
    re1, im1, re2, im2 = re1 * f1, im1 * f1, re2 * f2, im2 * f2
    return re1 + re2, im1 + im2, im1 - im2, re2 - re1


def cut_maps(cuts, level, shape, low_rows, low_cols):
    row_low = lax.broadcasted_iota(jnp.int32, shape, 0) < low_rows
    col_low = lax.broadcasted_iota(jnp.int32, shape, 1) < low_cols
    pick = []
    for k in range(2):
        lh, hl, hh = (cuts[level, 2 * o + k].astype(jnp.float32) / 32.0 for o in range(3))
        pick.append(jnp.where(row_low, lh, jnp.where(col_low, hl, hh)))
    return pick[0], pick[1], jnp.logical_and(row_low, col_low)


def packed(matrix):
    hi, lo = halves(matrix)
    return np.concatenate(
        [np.concatenate([hi, hi], -1), np.concatenate([lo, np.zeros_like(lo)], -1)], -2
    )


def by_rows(x, weight):
    y = dot(jnp.concatenate(split(x), 1), weight, True)
    half = weight.shape[0] // 2
    return y[:, :half] + y[:, half:]


def by_cols(weight, x):
    y = dot(weight, jnp.concatenate(split(x), 0), False)
    half = weight.shape[0] // 2
    return y[:half] + y[half:]


def both_ways(bands, chan_weight, time_weight):
    rows, cols = bands[0].shape
    timed = []
    for q in range(2):
        timed.append(by_rows(jnp.concatenate([bands[q], bands[2 + q]], 0), time_weight[q]))
    out = []
    for p in range(2):
        part = slice(p * rows, (p + 1) * rows)
        y = by_cols(chan_weight[p], jnp.concatenate([timed[0][part], timed[1][part]], 1))
        out += [y[:, :cols], y[:, cols:]]
    return out


def denoise(cuts, slab, sources, tables, picked, cleaned, coefs):
    c1, c1t, t1, c2, c2t, t2, t2t, c3, c3t, t3, t3t = tables
    trees = [(0, 0), (0, 1), (1, 0), (1, 1)]
    rows = slab.shape[1]
    cols = 2 * BLOCK
    x = split(jnp.concatenate([slab[0], slab[1]], 1))
    first = split(dot3(x, (t1[0], t1[1]), True))
    coefs[...] = dot3((c1[0], c1[1]), first)
    hr, hc = rows // 2, cols // 2
    corners = [
        (slice(p * rows, p * rows + hr), slice(q * cols, q * cols + hc)) for p, q in trees
    ]
    lows = both_ways([coefs[a, b] for a, b in corners], c2, t2)
    deep = both_ways(lows, c3, t3)
    live = hr // 2
    deep = [band[:live] for band in deep]
    one, two, kept = cut_maps(cuts, 2, deep[0].shape, hr // 4, hc // 4)
    shrunk = shrink(*deep, one, two)
    deep = [jnp.where(kept, a, b) for a, b in zip(deep, shrunk)]
    rest = jnp.zeros((hr - live, hc), jnp.float32)
    inner = both_ways([jnp.concatenate([band, rest], 0) for band in deep], c3t, t3t)
    one, two, kept = cut_maps(cuts, 1, lows[0].shape, hr // 2, hc // 2)
    shrunk = shrink(*lows, one, two)
    outer = both_ways([jnp.where(kept, a, b) for a, b in zip(inner, shrunk)], c2t, t2t)
    for orient, (row_high, col_high) in enumerate([(0, 1), (1, 0), (1, 1)]):
        spots = [
            (
                slice(p * rows + row_high * hr, p * rows + row_high * hr + hr),
                slice(q * cols + col_high * hc, q * cols + col_high * hc + hc),
            )
            for p, q in trees
        ]
        top = [
            cuts[0, 2 * orient + k].astype(jnp.float32) / 32.0 for k in range(2)
        ]
        done = shrink(*[coefs[a, b] for a, b in spots], top[0], top[1])
        for (a, b), cell in zip(spots, done):
            coefs[a, b] = cell
    for (a, b), band in zip(corners, outer):
        coefs[a, b] = band
    hi, lo = split(coefs[...])
    t_hi, t_lo = t1[0, :, :BLOCK], t1[1, :, :BLOCK]
    y = dot(hi, jnp.concatenate([t_hi, t_lo], 1), False)
    timed = jnp.concatenate(split(y[:, :BLOCK] + y[:, BLOCK:] + dot(lo, t_hi, False)), 1)
    y = dot(c1t[0], timed, False)
    whole = y[:, :BLOCK] + y[:, BLOCK:] + dot(c1t[1], timed[:, :BLOCK], False)
    result = (0.25 * whole).astype(jnp.bfloat16)
    cleaned[...] = result.astype(jnp.float32).reshape(rows // 8, 8, BLOCK).astype(jnp.bfloat16)
    one_hot = jnp.where(
        lax.broadcasted_iota(jnp.int32, (rows, sources.shape[1]), 0) == sources[...], 1.0, 0.0
    )
    chosen = jnp.transpose(one_hot).astype(jnp.bfloat16)
    picked[...] = dot(chosen, result, False).astype(jnp.bfloat16)


def spread(picks, cleaned, receivers, near, far, across, recv, send, land, own):
    n_chan, n_tm = lax.axis_size("chan"), lax.axis_size("tm")
    c, t = lax.axis_index("chan"), lax.axis_index("tm")
    blocks = picks.shape[0]
    count = blocks // n_tm
    rep = n_chan // count
    pairs = n_tm // 2
    share = cleaned.shape[0] * 8 // (n_chan * n_tm)
    place, copy_index, core = c // rep, lax.rem(c, rep), lax.rem(t, 2)
    mine = t * count + place

    def move(block, sem, chan, tm):
        return pltpu.make_async_remote_copy(
            src_ref=picks.at[block],
            dst_ref=picks.at[block],
            send_sem=sem,
            recv_sem=recv.at[block],
            device_id=(chan, tm),
            device_id_type=MESH,
        )

    def group(k):
        return move(mine, near.at[k], lax.rem(place + k, count) * rep + copy_index, t)

    def along(u, k):
        block = t * count + lax.rem(place + count - k, count)
        to = lax.rem(t // 2 + u, pairs) * 2 + core
        return move(block, far.at[u * count + k], c, to)

    def beside(u, k):
        other = lax.rem(t // 2 + pairs - u, pairs) * 2 + core
        block = other * count + lax.rem(place + count - k, count)
        return move(block, across.at[u * count + k], c, t + 1 - 2 * core)

    def rows_of(dc, dt):
        return (dc * n_tm + dt) * share // 8

    def personal(k):
        dc = lax.rem(place + k // n_tm, count) * rep + copy_index
        dt = lax.rem(t + lax.rem(k, n_tm), n_tm)
        return pltpu.make_async_remote_copy(
            src_ref=cleaned.at[rows_of(dc, dt)],
            dst_ref=receivers.at[mine],
            send_sem=send.at[k],
            recv_sem=land.at[mine],
            device_id=(dc, dt),
            device_id_type=MESH,
        )

    def each(low, high, act):
        def body(k, carry):
            act(k)
            return carry

        lax.fori_loop(low, high, body, 0)

    def await_block(block):
        move(block, near.at[0], c, t + 1 - 2 * core).wait_recv()

    def relay(k):
        @pl.when(k > 0)
        def _():
            await_block(t * count + lax.rem(place + count - k, count))

        for u in range(1, pairs):
            along(u, k).start()
        beside(0, k).start()

    each(1, count, lambda k: group(k).start())
    local = pltpu.make_async_copy(cleaned.at[rows_of(c, t)], receivers.at[mine], own)
    local.start()
    relay(0)
    each(1, blocks, lambda k: personal(k).start())
    each(1, count, relay)
    for u in range(1, pairs):

        def cross_over(k, u=u):
            other = lax.rem(t // 2 + pairs - u, pairs) * 2 + core
            await_block(other * count + lax.rem(place + count - k, count))
            beside(u, k).start()

        each(0, count, cross_over)
    for u in range(pairs):

        def last(k, u=u):
            other = lax.rem(t // 2 + pairs - u, pairs) * 2 + 1 - core
            await_block(other * count + lax.rem(place + count - k, count))

        each(0, count, last)

    def landed(k):
        block = lax.rem(mine + k, blocks)
        pltpu.make_async_remote_copy(
            src_ref=cleaned.at[0],
            dst_ref=receivers.at[block],
            send_sem=send.at[0],
            recv_sem=land.at[block],
            device_id=(c, t + 1 - 2 * core),
            device_id_type=MESH,
        ).wait_recv()

    local.wait()
    each(1, blocks, landed)
    each(1, count, lambda k: group(k).wait_send())
    each(1, blocks, lambda k: personal(k).wait_send())
    for u in range(pairs):
        each(0, count, lambda k, u=u: beside(u, k).wait_send())
        if u:
            each(0, count, lambda k, u=u: along(u, k).wait_send())


def clean_kernel(n_tables, same, cuts, samples, sources, *refs):
    stored, refs = refs[:n_tables], refs[n_tables:]
    picks, receivers = refs[:2]
    held, refs = refs[2 : 2 + n_tables], refs[2 + n_tables :]
    slab, blocks, edge, coefs, cleaned, loads = refs[:6]
    gather_sems, spread_sems = refs[6:11], refs[11:]
    copies = [pltpu.make_async_copy(a, b, loads.at[i]) for i, (a, b) in enumerate(zip(stored, held))]
    for copy in copies:
        copy.start()
    gather(samples, slab, blocks, edge, *gather_sems)
    for copy in copies:
        copy.wait()
    c1t, t1, c2, c2t, c3, c3t = held[:6]
    extra = [t1, c2, c2t, c3, c3t] if same else held[6:]
    tables = [extra[0], c1t, t1, extra[1], extra[2], c2, c2t, extra[3], extra[4], c3, c3t]
    n_tm = lax.axis_size("tm")
    count = picks.shape[0] // n_tm
    rep = lax.axis_size("chan") // count
    mine = lax.axis_index("tm") * count + lax.axis_index("chan") // rep
    denoise(cuts, slab, sources, tables, picks.at[mine], cleaned, coefs)
    spread(picks, cleaned, receivers, *spread_sems)


def correlate_kernel(picks, receivers, table, out, white, heard, cross):
    per_window = N // BLOCK
    windows, sources = picks.shape[0] // per_window, picks.shape[1]

    def window(ref, w):
        return jnp.concatenate([ref[w * per_window + j] for j in range(per_window)], 1)

    def whiten(block):
        spectra = dot(block, table[...], False)
        scale = lax.rsqrt(jnp.mean(spectra * spectra, axis=1, keepdims=True) + 1e-05)
        return (spectra * scale).astype(jnp.bfloat16).astype(jnp.float32)

    heard_rows = [window(receivers, w).astype(jnp.float32) for w in range(windows)]
    joined = jnp.concatenate(
        [window(picks, w) for w in range(windows)]
        + [jnp.concatenate(heard_rows, 0).astype(jnp.bfloat16)],
        0,
    )
    spectra = whiten(joined)
    base = windows * sources
    for part in range(N // BLOCK):
        white[part] = spectra[:base, BLOCK * part : BLOCK * (part + 1)]
    for w in range(windows):
        heard[w] = spectra[base + 8 * w : base + 8 * w + 8]
    weight = jnp.where(lax.broadcasted_iota(jnp.int32, (1, BLOCK), 1) == 0, 1.0, 2.0)

    def body(g, carry):
        for chunk in range(BINS // BLOCK):
            lo = chunk * BLOCK
            hi = BINS + lo
            real = [None, None]
            imag = [None, None]
            for w in range(windows):
                rr = heard[w, :, lo : lo + BLOCK]
                ri = heard[w, :, hi : hi + BLOCK]
                for j in range(2):
                    spread = pl.ds(w * sources + 2 * g + j, 8, stride=0)
                    pr = white.at[chunk][spread, :]
                    pi = white.at[chunk + BINS // BLOCK][spread, :]
                    a = pr * rr + pi * ri
                    b = pi * rr - pr * ri
                    real[j] = a if real[j] is None else real[j] + a
                    imag[j] = b if imag[j] is None else imag[j] + b
            factor = weight if chunk == 0 else 2.0
            spot = pl.ds(pl.multiple_of(16 * g, 16), 16)
            cross[spot, lo : lo + BLOCK] = (jnp.concatenate(real, 0) * factor).astype(jnp.bfloat16)
            cross[spot, hi : hi + BLOCK] = (jnp.concatenate(imag, 0) * factor).astype(jnp.bfloat16)
        return carry

    lax.fori_loop(0, sources // 2, body, 0)
    scale = 1.0 / math.sqrt(windows * N)
    half = LAGS // 2
    lags = jnp.concatenate([table[N - half :, :], table[:half, :]], 0)
    out[...] = dot(cross[...], lags, True) * scale


def local(samples, thresholds, sources):
    n_chan, n_tm = lax.axis_size("chan"), lax.axis_size("tm")
    rows, width = samples.shape
    channels = rows * n_chan
    count = width // BLOCK
    rep = n_chan // count
    blocks = count * n_tm
    windows = n_tm * width // N
    picked_count = sources.shape[0]
    vmem = pl.BlockSpec(memory_space=pltpu.VMEM)
    smem = pl.BlockSpec(memory_space=pltpu.SMEM)
    dma = pltpu.SemaphoreType.DMA
    f32, bf16 = jnp.float32, jnp.bfloat16
    big = 60 * 1024 * 1024

    def wide(matrix):
        return halves(matrix.reshape(-1, matrix.shape[-1]))

    def flipped(matrix):
        return np.swapaxes(matrix, -1, -2)

    def cornered(matrix):
        size = matrix.shape[-1]
        return np.pad(matrix, ((0, 0), (0, size), (0, size)))

    def pack_pair(length):
        second, third = bank_matrix(length // 2), cornered(bank_matrix(length // 4))
        return [packed(m) for m in (second, flipped(second), third, flipped(third))]

    same = channels == 2 * BLOCK
    c1, t1 = wide(bank_matrix(channels)), wide(bank_matrix(2 * BLOCK))
    chan, time = pack_pair(channels), pack_pair(2 * BLOCK)
    tables = [np.ascontiguousarray(flipped(c1)), t1, *time]
    if not same:
        tables += [c1, *chan]

    far_count = blocks // 2
    picks, receivers = pl.pallas_call(
        functools.partial(clean_kernel, len(tables), same),
        out_shape=(
            jax.ShapeDtypeStruct((blocks, picked_count, BLOCK), bf16),
            jax.ShapeDtypeStruct((blocks, 8, BLOCK), bf16),
        ),
        in_specs=[smem, vmem, vmem] + [pl.BlockSpec(memory_space=pl.ANY)] * len(tables),
        out_specs=(vmem, vmem),
        scratch_shapes=[pltpu.VMEM(a.shape, bf16) for a in tables]
        + [
            pltpu.VMEM((2, channels, BLOCK), f32),
            pltpu.VMEM((2 * count + 1, rows, BLOCK), f32),
            pltpu.VMEM((channels, BLOCK), f32),
            pltpu.VMEM((2 * channels, 4 * BLOCK), f32),
            pltpu.VMEM((channels // 8, 8, BLOCK), bf16),
            dma((len(tables),)),
            dma((n_chan,)),
            dma((n_chan,)),
            dma((2 * rep,)),
            dma((n_chan,)),
            dma,
            dma((count,)),
            dma((far_count,)),
            dma((far_count,)),
            dma((blocks,)),
            dma((blocks,)),
            dma((blocks,)),
            dma,
        ],
        compiler_params=pltpu.CompilerParams(
            collective_id=0, has_side_effects=True, vmem_limit_bytes=big
        ),
        name="clean",
    )(thresholds, samples, sources[None, :], *[jnp.asarray(a) for a in tables])

    out = pl.pallas_call(
        correlate_kernel,
        out_shape=jax.ShapeDtypeStruct((picked_count * 8, LAGS), f32),
        in_specs=[vmem] * 3,
        out_specs=vmem,
        scratch_shapes=[
            pltpu.VMEM((N // BLOCK, windows * picked_count, BLOCK), f32),
            pltpu.VMEM((windows, 8, N), f32),
            pltpu.VMEM((picked_count * 8, N), bf16),
        ],
        compiler_params=pltpu.CompilerParams(vmem_limit_bytes=big),
        name="correlate",
    )(picks, receivers, jnp.asarray(dft_table()))
    out = out.reshape(picked_count, 8, LAGS)
    share = channels // (n_chan * n_tm)
    if share < 8:
        place = lax.axis_index("chan") * n_tm + lax.axis_index("tm")
        out = lax.dynamic_slice_in_dim(out, lax.rem(place * share, 8), share, 1)
    return out


def solution(mesh):
    return jax.shard_map(
        local,
        mesh=mesh,
        in_specs=(P("chan", "tm"), P(), P()),
        out_specs=P(None, ("chan", "tm"), None),
        check_vma=False,
    )
```

```python
import functools
import math

import jax
import jax.numpy as jnp
import numpy as np
from jax import lax
from jax.experimental import pallas as pl
from jax.experimental.pallas import tpu as pltpu
from jax.sharding import PartitionSpec as P

N = 1024
LEVELS = 3
BINS = 512
LAGS = 512
BLOCK = 128
HALF = 64
MESH = pl.DeviceIdType.MESH

daubechies = [
    0.2303778133088964,
    0.7148465705529155,
    0.6308807679298587,
    -0.0279837694168599,
    -0.1870348117190931,
    0.0308413818355607,
    0.0328830116668852,
    -0.010597401785069,
]


def filter_bank():
    lowpass = list(daubechies)
    highpass = [(1.0 if k % 2 == 0 else -1.0) * daubechies[7 - k] for k in range(8)]
    return [(lowpass, highpass), (lowpass[::-1], highpass[::-1])]


def bank_matrix(length):
    half = length // 2
    out = np.zeros((2, 2, half, length))
    rows = np.arange(half)
    for tree, pair in enumerate(filter_bank()):
        for band, taps in enumerate(pair):
            for k in range(8):
                np.add.at(out[tree, band], (rows, (2 * rows + k - 3) % length), taps[k])
    return out.reshape(2, length, length)


def halves(matrix):
    m32 = np.asarray(matrix, np.float32)
    hi = m32.astype(jnp.bfloat16)
    lo = (m32 - hi.astype(np.float32)).astype(jnp.bfloat16)
    return np.stack([hi, lo])


def dft_table():
    t = np.arange(N)
    f = np.arange(BINS)
    phases = ((t[:, None] * f[None, :]) % N).astype(np.float64) * (2.0 * math.pi / N)
    table = np.concatenate([np.cos(phases), -np.sin(phases)], 1)
    return table.astype(np.float32).astype(jnp.bfloat16)


def split(x):
    hi = x.astype(jnp.bfloat16)
    lo = (x - hi.astype(jnp.float32)).astype(jnp.bfloat16)
    return hi, lo


def dot(a, b, trans_b):
    dims = (((1,), (1 if trans_b else 0,)), ((), ()))
    return lax.dot_general(a, b, dims, preferred_element_type=jnp.float32)


def dot3(a, b, trans_b=False):
    return dot(a[0], b[0], trans_b) + (dot(a[1], b[0], trans_b) + dot(a[0], b[1], trans_b))


def greet_all():
    n_tm = lax.axis_size("tm")
    n = lax.axis_size("chan") * n_tm
    me = lax.axis_index("chan") * n_tm + lax.axis_index("tm")
    barrier = pltpu.get_barrier_semaphore()

    def greet(k, carry):
        d = lax.rem(me + k, n)
        pl.semaphore_signal(
            barrier, inc=1, device_id=(d // n_tm, lax.rem(d, n_tm)), device_id_type=MESH
        )
        return carry

    lax.fori_loop(1, n, greet, 0)
    pl.semaphore_wait(barrier, n - 1)


def gather(
    samples, slab, rim_slab, blocks, rims, edge, send, recv, edge_send, edge_recv
):
    n_chan, n_tm = lax.axis_size("chan"), lax.axis_size("tm")
    c, t = lax.axis_index("chan"), lax.axis_index("tm")
    rows, width = samples.shape
    count = width // BLOCK
    rep = n_chan // count
    values = samples[...]
    for j in range(count):
        right, left = (BLOCK * (j + 1)) % width, (BLOCK * j - HALF) % width
        blocks[j] = values[:, BLOCK * j : BLOCK * (j + 1)]
        rims[j] = jnp.concatenate(
            [values[:, right : right + HALF], values[:, left : left + HALF]], 1
        ).astype(jnp.bfloat16)
    rims[count] = jnp.concatenate([values[:, :HALF], values[:, width - HALF :]], 1).astype(
        jnp.bfloat16
    )
    greet_all()
    mine = pl.ds(pl.multiple_of(c * rows, rows), rows)
    place = c // rep

    def pair(to, rows_at, landing):
        return (
            pltpu.make_async_remote_copy(
                src_ref=blocks.at[to // rep],
                dst_ref=slab.at[rows_at, :],
                send_sem=send.at[to],
                recv_sem=recv.at[landing],
                device_id=(to, t),
                device_id_type=MESH,
            ),
            pltpu.make_async_remote_copy(
                src_ref=rims.at[to // rep],
                dst_ref=rim_slab.at[rows_at, :],
                send_sem=send.at[n_chan + to],
                recv_sem=recv.at[n_chan + landing],
                device_id=(to, t),
                device_id_type=MESH,
            ),
        )

    def remote(to):
        return pair(to, mine, c)

    def incoming(source):
        return pair(source, pl.ds(pl.multiple_of(source * rows, rows), rows), source)

    def rim(to, shift, r):
        return pltpu.make_async_remote_copy(
            src_ref=rims.at[count],
            dst_ref=edge.at[mine, :],
            send_sem=edge_send.at[r],
            recv_sem=edge_recv.at[c],
            device_id=(to, lax.rem(t + shift, n_tm)),
            device_id_type=MESH,
        )

    for r in range(rep):
        rim(r, 1, r).start()
        rim((count - 1) * rep + r, n_tm - 1, rep + r).start()
    slab[mine, :] = blocks[place]
    rim_slab[mine, :] = rims[place]

    def start(k, carry):
        for copy in remote(lax.rem(c + k, n_chan)):
            copy.start()
        return carry

    lax.fori_loop(1, n_chan, start, 0)

    def finish(k, carry):
        for copy in incoming(lax.rem(c + n_chan - k, n_chan)):
            copy.wait_recv()
        return carry

    lax.fori_loop(1, n_chan, finish, 0)
    at_edge = jnp.logical_or(place == 0, place == count - 1)

    @pl.when(at_edge)
    def _():
        def take(source, carry):
            pltpu.make_async_remote_copy(
                src_ref=rims.at[count],
                dst_ref=edge.at[pl.ds(pl.multiple_of(source * rows, rows), rows), :],
                send_sem=edge_send.at[0],
                recv_sem=edge_recv.at[source],
                device_id=(source, lax.rem(t + 1, n_tm)),
                device_id_type=MESH,
            ).wait_recv()
            return carry

        lax.fori_loop(0, n_chan, take, 0)

    left = lax.broadcasted_iota(jnp.int32, edge.shape, 1) < HALF

    @pl.when(place == 0)
    def _():
        rim_slab[...] = jnp.where(left, rim_slab[...], edge[...])

    @pl.when(place == count - 1)
    def _():
        rim_slab[...] = jnp.where(left, edge[...], rim_slab[...])

    def sent(k, carry):
        for copy in remote(lax.rem(c + k, n_chan)):
            copy.wait_send()
        return carry

    lax.fori_loop(1, n_chan, sent, 0)
    for r in range(rep):
        rim(r, 1, r).wait_send()
        rim((count - 1) * rep + r, n_tm - 1, rep + r).wait_send()


def shrink(aa, ab, ba, bb, cut_one, cut_two):
    root_half = 1.0 / math.sqrt(2.0)
    re1 = (aa - bb) * root_half
    im1 = (ab + ba) * root_half
    re2 = (aa + bb) * root_half
    im2 = (ab - ba) * root_half
    f1 = jnp.maximum(1.0 - cut_one * lax.rsqrt(re1 * re1 + im1 * im1), 0.0) * root_half
    f2 = jnp.maximum(1.0 - cut_two * lax.rsqrt(re2 * re2 + im2 * im2), 0.0) * root_half
    re1, im1, re2, im2 = re1 * f1, im1 * f1, re2 * f2, im2 * f2
    return re1 + re2, im1 + im2, im1 - im2, re2 - re1


def cut_maps(cuts, level, shape, low_rows, low_cols):
    row_low = lax.broadcasted_iota(jnp.int32, shape, 0) < low_rows
    col_low = lax.broadcasted_iota(jnp.int32, shape, 1) < low_cols
    pick = []
    for k in range(2):
        lh, hl, hh = (cuts[level, 2 * o + k].astype(jnp.float32) / 32.0 for o in range(3))
        pick.append(jnp.where(row_low, lh, jnp.where(col_low, hl, hh)))
    return pick[0], pick[1], jnp.logical_and(row_low, col_low)


def packed(matrix):
    hi, lo = halves(matrix)
    return np.concatenate(
        [np.concatenate([hi, hi], -1), np.concatenate([lo, np.zeros_like(lo)], -1)], -2
    )


def by_rows(x, weight):
    y = dot(jnp.concatenate(split(x), 1), weight, True)
    half = weight.shape[0] // 2
    return y[:, :half] + y[:, half:]


def by_cols(weight, x):
    y = dot(weight, jnp.concatenate(split(x), 0), False)
    half = weight.shape[0] // 2
    return y[:half] + y[half:]


def both_ways(bands, chan_weight, time_weight):
    rows, cols = bands[0].shape
    timed = []
    for q in range(2):
        timed.append(by_rows(jnp.concatenate([bands[q], bands[2 + q]], 0), time_weight[q]))
    out = []
    for p in range(2):
        part = slice(p * rows, (p + 1) * rows)
        y = by_cols(chan_weight[p], jnp.concatenate([timed[0][part], timed[1][part]], 1))
        out += [y[:, :cols], y[:, cols:]]
    return out


def denoise(cuts, slab, rim_slab, sources, tables, picked, cleaned, coefs):
    c1, c1t, t1, c2, c2t, t2, t2t, c3, c3t, t3, t3t = tables
    trees = [(0, 0), (0, 1), (1, 0), (1, 1)]
    rows = slab.shape[0]
    cols = 2 * BLOCK
    hi, lo = split(slab[...])
    rim = rim_slab[...]
    x = jnp.concatenate([hi, rim], 1), jnp.concatenate([lo, jnp.zeros_like(rim)], 1)
    first = split(dot3(x, (t1[0], t1[1]), True))
    coefs[...] = dot3((c1[0], c1[1]), first)
    hr, hc = rows // 2, cols // 2
    corners = [
        (slice(p * rows, p * rows + hr), slice(q * cols, q * cols + hc)) for p, q in trees
    ]
    lows = both_ways([coefs[a, b] for a, b in corners], c2, t2)
    deep = both_ways(lows, c3, t3)
    live = hr // 2
    deep = [band[:live] for band in deep]
    one, two, kept = cut_maps(cuts, 2, deep[0].shape, hr // 4, hc // 4)
    shrunk = shrink(*deep, one, two)
    deep = [jnp.where(kept, a, b) for a, b in zip(deep, shrunk)]
    rest = jnp.zeros((hr - live, hc), jnp.float32)
    inner = both_ways([jnp.concatenate([band, rest], 0) for band in deep], c3t, t3t)
    one, two, kept = cut_maps(cuts, 1, lows[0].shape, hr // 2, hc // 2)
    shrunk = shrink(*lows, one, two)
    outer = both_ways([jnp.where(kept, a, b) for a, b in zip(inner, shrunk)], c2t, t2t)
    for orient, (row_high, col_high) in enumerate([(0, 1), (1, 0), (1, 1)]):
        spots = [
            (
                slice(p * rows + row_high * hr, p * rows + row_high * hr + hr),
                slice(q * cols + col_high * hc, q * cols + col_high * hc + hc),
            )
            for p, q in trees
        ]
        top = [
            cuts[0, 2 * orient + k].astype(jnp.float32) / 32.0 for k in range(2)
        ]
        done = shrink(*[coefs[a, b] for a, b in spots], top[0], top[1])
        for (a, b), cell in zip(spots, done):
            coefs[a, b] = cell
    for (a, b), band in zip(corners, outer):
        coefs[a, b] = band
    hi, lo = split(coefs[...])
    t_hi, t_lo = t1[0, :, :BLOCK], t1[1, :, :BLOCK]
    y = dot(hi, jnp.concatenate([t_hi, t_lo], 1), False)
    timed = jnp.concatenate(split(y[:, :BLOCK] + y[:, BLOCK:] + dot(lo, t_hi, False)), 1)
    y = dot(c1t[0], timed, False)
    whole = y[:, :BLOCK] + y[:, BLOCK:] + dot(c1t[1], timed[:, :BLOCK], False)
    result = (0.25 * whole).astype(jnp.bfloat16)
    cleaned[...] = result.astype(jnp.float32).reshape(rows // 8, 8, BLOCK).astype(jnp.bfloat16)
    one_hot = jnp.where(
        lax.broadcasted_iota(jnp.int32, (rows, sources.shape[1]), 0) == sources[...], 1.0, 0.0
    )
    chosen = jnp.transpose(one_hot).astype(jnp.bfloat16)
    picked[...] = dot(chosen, result, False).astype(jnp.bfloat16)


def spread(picks, cleaned, receivers, near, far, across, recv, send, land, own):
    n_chan, n_tm = lax.axis_size("chan"), lax.axis_size("tm")
    c, t = lax.axis_index("chan"), lax.axis_index("tm")
    blocks = picks.shape[0]
    count = blocks // n_tm
    rep = n_chan // count
    pairs = n_tm // 2
    share = cleaned.shape[0] * 8 // (n_chan * n_tm)
    place, copy_index, core = c // rep, lax.rem(c, rep), lax.rem(t, 2)
    mine = t * count + place

    def move(block, sem, chan, tm):
        return pltpu.make_async_remote_copy(
            src_ref=picks.at[block],
            dst_ref=picks.at[block],
            send_sem=sem,
            recv_sem=recv.at[block],
            device_id=(chan, tm),
            device_id_type=MESH,
        )

    def group(k):
        return move(mine, near.at[k], lax.rem(place + k, count) * rep + copy_index, t)

    def along(u, k):
        block = t * count + lax.rem(place + count - k, count)
        to = lax.rem(t // 2 + u, pairs) * 2 + core
        return move(block, far.at[u * count + k], c, to)

    def beside(u, k):
        other = lax.rem(t // 2 + pairs - u, pairs) * 2 + core
        block = other * count + lax.rem(place + count - k, count)
        return move(block, across.at[u * count + k], c, t + 1 - 2 * core)

    def rows_of(dc, dt):
        return (dc * n_tm + dt) * share // 8

    def personal(k):
        dc = lax.rem(place + k // n_tm, count) * rep + copy_index
        dt = lax.rem(t + lax.rem(k, n_tm), n_tm)
        return pltpu.make_async_remote_copy(
            src_ref=cleaned.at[rows_of(dc, dt)],
            dst_ref=receivers.at[mine],
            send_sem=send.at[k],
            recv_sem=land.at[mine],
            device_id=(dc, dt),
            device_id_type=MESH,
        )

    def each(low, high, act):
        def body(k, carry):
            act(k)
            return carry

        lax.fori_loop(low, high, body, 0)

    def await_block(block):
        move(block, near.at[0], c, t + 1 - 2 * core).wait_recv()

    def relay(k):
        @pl.when(k > 0)
        def _():
            await_block(t * count + lax.rem(place + count - k, count))

        for u in range(1, pairs):
            along(u, k).start()
        beside(0, k).start()

    each(1, count, lambda k: group(k).start())
    local = pltpu.make_async_copy(cleaned.at[rows_of(c, t)], receivers.at[mine], own)
    local.start()
    relay(0)
    each(1, blocks, lambda k: personal(k).start())
    each(1, count, relay)
    for u in range(1, pairs):

        def cross_over(k, u=u):
            other = lax.rem(t // 2 + pairs - u, pairs) * 2 + core
            await_block(other * count + lax.rem(place + count - k, count))
            beside(u, k).start()

        each(0, count, cross_over)
    for u in range(pairs):

        def last(k, u=u):
            other = lax.rem(t // 2 + pairs - u, pairs) * 2 + 1 - core
            await_block(other * count + lax.rem(place + count - k, count))

        each(0, count, last)

    def landed(k):
        block = lax.rem(mine + k, blocks)
        pltpu.make_async_remote_copy(
            src_ref=cleaned.at[0],
            dst_ref=receivers.at[block],
            send_sem=send.at[0],
            recv_sem=land.at[block],
            device_id=(c, t + 1 - 2 * core),
            device_id_type=MESH,
        ).wait_recv()

    local.wait()
    each(1, blocks, landed)
    each(1, count, lambda k: group(k).wait_send())
    each(1, blocks, lambda k: personal(k).wait_send())
    for u in range(pairs):
        each(0, count, lambda k, u=u: beside(u, k).wait_send())
        if u:
            each(0, count, lambda k, u=u: along(u, k).wait_send())


def whole_kernel(n_tables, same, cuts, samples, sources, *refs):
    stored, refs = refs[:n_tables], refs[n_tables:]
    out, picks, receivers, white, heard, cross = refs[:6]
    held, refs = refs[6 : 6 + n_tables], refs[6 + n_tables :]
    slab, rim_slab, blocks, rims, edge, coefs, cleaned, loads = refs[:8]
    gather_sems, spread_sems = refs[8:12], refs[12:]
    copies = [pltpu.make_async_copy(a, b, loads.at[i]) for i, (a, b) in enumerate(zip(stored, held))]
    for copy in copies:
        copy.start()
    gather(samples, slab, rim_slab, blocks, rims, edge, *gather_sems)
    for copy in copies[:-1]:
        copy.wait()
    c1t, t1, c2, c2t, c3, c3t = held[:6]
    extra = [t1, c2, c2t, c3, c3t] if same else held[6:-1]
    tables = [extra[0], c1t, t1, extra[1], extra[2], c2, c2t, extra[3], extra[4], c3, c3t]
    n_tm = lax.axis_size("tm")
    count = picks.shape[0] // n_tm
    rep = lax.axis_size("chan") // count
    mine = lax.axis_index("tm") * count + lax.axis_index("chan") // rep
    denoise(cuts, slab, rim_slab, sources, tables, picks.at[mine], cleaned, coefs)
    spread(picks, cleaned, receivers, *spread_sems)
    copies[-1].wait()
    correlate(picks, receivers, held[-1], out, white, heard, cross)


def correlate(picks, receivers, table, out, white, heard, cross):
    per_window = N // BLOCK
    windows, sources = picks.shape[0] // per_window, picks.shape[1]

    def window(ref, w):
        return jnp.concatenate([ref[w * per_window + j] for j in range(per_window)], 1)

    def whiten(block):
        spectra = dot(block, table[...], False)
        scale = lax.rsqrt(jnp.mean(spectra * spectra, axis=1, keepdims=True) + 1e-05)
        return (spectra * scale).astype(jnp.bfloat16).astype(jnp.float32)

    heard_rows = [window(receivers, w).astype(jnp.float32) for w in range(windows)]
    joined = jnp.concatenate(
        [window(picks, w) for w in range(windows)]
        + [jnp.concatenate(heard_rows, 0).astype(jnp.bfloat16)],
        0,
    )
    spectra = whiten(joined)
    base = windows * sources
    for part in range(N // BLOCK):
        white[part] = spectra[:base, BLOCK * part : BLOCK * (part + 1)]
    for w in range(windows):
        heard[w] = spectra[base + 8 * w : base + 8 * w + 8]
    weight = jnp.where(lax.broadcasted_iota(jnp.int32, (1, BLOCK), 1) == 0, 1.0, 2.0)

    def body(g, carry):
        for chunk in range(BINS // BLOCK):
            lo = chunk * BLOCK
            hi = BINS + lo
            real = [None, None]
            imag = [None, None]
            for w in range(windows):
                rr = heard[w, :, lo : lo + BLOCK]
                ri = heard[w, :, hi : hi + BLOCK]
                for j in range(2):
                    spread = pl.ds(w * sources + 2 * g + j, 8, stride=0)
                    pr = white.at[chunk][spread, :]
                    pi = white.at[chunk + BINS // BLOCK][spread, :]
                    a = pr * rr + pi * ri
                    b = pi * rr - pr * ri
                    real[j] = a if real[j] is None else real[j] + a
                    imag[j] = b if imag[j] is None else imag[j] + b
            factor = weight if chunk == 0 else 2.0
            spot = pl.ds(pl.multiple_of(16 * g, 16), 16)
            cross[spot, lo : lo + BLOCK] = (jnp.concatenate(real, 0) * factor).astype(jnp.bfloat16)
            cross[spot, hi : hi + BLOCK] = (jnp.concatenate(imag, 0) * factor).astype(jnp.bfloat16)
        return carry

    lax.fori_loop(0, sources // 2, body, 0)
    scale = 1.0 / math.sqrt(windows * N)
    half = LAGS // 2
    lags = jnp.concatenate([table[N - half :, :], table[:half, :]], 0)
    out[...] = dot(cross[...], lags, True) * scale


def local(samples, thresholds, sources):
    n_chan, n_tm = lax.axis_size("chan"), lax.axis_size("tm")
    rows, width = samples.shape
    channels = rows * n_chan
    count = width // BLOCK
    rep = n_chan // count
    blocks = count * n_tm
    windows = n_tm * width // N
    picked_count = sources.shape[0]
    vmem = pl.BlockSpec(memory_space=pltpu.VMEM)
    smem = pl.BlockSpec(memory_space=pltpu.SMEM)
    dma = pltpu.SemaphoreType.DMA
    f32, bf16 = jnp.float32, jnp.bfloat16
    big = 60 * 1024 * 1024

    def wide(matrix):
        return halves(matrix.reshape(-1, matrix.shape[-1]))

    def flipped(matrix):
        return np.swapaxes(matrix, -1, -2)

    def cornered(matrix):
        size = matrix.shape[-1]
        return np.pad(matrix, ((0, 0), (0, size), (0, size)))

    def pack_pair(length):
        second, third = bank_matrix(length // 2), cornered(bank_matrix(length // 4))
        return [packed(m) for m in (second, flipped(second), third, flipped(third))]

    same = channels == 2 * BLOCK
    c1, t1 = wide(bank_matrix(channels)), wide(bank_matrix(2 * BLOCK))
    chan, time = pack_pair(channels), pack_pair(2 * BLOCK)
    tables = [np.ascontiguousarray(flipped(c1)), t1, *time]
    if not same:
        tables += [c1, *chan]
    tables.append(dft_table())

    far_count = blocks // 2
    out = pl.pallas_call(
        functools.partial(whole_kernel, len(tables), same),
        out_shape=jax.ShapeDtypeStruct((picked_count * 8, LAGS), f32),
        in_specs=[smem, vmem, vmem] + [pl.BlockSpec(memory_space=pl.ANY)] * len(tables),
        out_specs=vmem,
        scratch_shapes=[
            pltpu.VMEM((blocks, picked_count, BLOCK), bf16),
            pltpu.VMEM((blocks, 8, BLOCK), bf16),
            pltpu.VMEM((N // BLOCK, windows * picked_count, BLOCK), f32),
            pltpu.VMEM((windows, 8, N), f32),
            pltpu.VMEM((picked_count * 8, N), bf16),
        ]
        + [pltpu.VMEM(a.shape, bf16) for a in tables]
        + [
            pltpu.VMEM((channels, BLOCK), f32),
            pltpu.VMEM((channels, BLOCK), bf16),
            pltpu.VMEM((count, rows, BLOCK), f32),
            pltpu.VMEM((count + 1, rows, BLOCK), bf16),
            pltpu.VMEM((channels, BLOCK), bf16),
            pltpu.VMEM((2 * channels, 4 * BLOCK), f32),
            pltpu.VMEM((channels // 8, 8, BLOCK), bf16),
            dma((len(tables),)),
            dma((2 * n_chan,)),
            dma((2 * n_chan,)),
            dma((2 * rep,)),
            dma((n_chan,)),
            dma((count,)),
            dma((far_count,)),
            dma((far_count,)),
            dma((blocks,)),
            dma((blocks,)),
            dma((blocks,)),
            dma,
        ],
        compiler_params=pltpu.CompilerParams(
            collective_id=0, has_side_effects=True, vmem_limit_bytes=big
        ),
        name="whole",
    )(thresholds, samples, sources[None, :], *[jnp.asarray(a) for a in tables])

    out = out.reshape(picked_count, 8, LAGS)
    share = channels // (n_chan * n_tm)
    if share < 8:
        place = lax.axis_index("chan") * n_tm + lax.axis_index("tm")
        out = lax.dynamic_slice_in_dim(out, lax.rem(place * share, 8), share, 1)
    return out


def solution(mesh):
    return jax.shard_map(
        local,
        mesh=mesh,
        in_specs=(P("chan", "tm"), P(), P()),
        out_specs=P(None, ("chan", "tm"), None),
        check_vma=False,
    )
```

```python
import functools
import math

import jax
import jax.numpy as jnp
import numpy as np
from jax import lax
from jax.experimental import pallas as pl
from jax.experimental.pallas import tpu as pltpu
from jax.sharding import PartitionSpec as P

N = 1024
LEVELS = 3
BINS = 512
LAGS = 512
BLOCK = 128
HALF = 64
MESH = pl.DeviceIdType.MESH

daubechies = [
    0.2303778133088964,
    0.7148465705529155,
    0.6308807679298587,
    -0.0279837694168599,
    -0.1870348117190931,
    0.0308413818355607,
    0.0328830116668852,
    -0.010597401785069,
]


def filter_bank():
    lowpass = list(daubechies)
    highpass = [(1.0 if k % 2 == 0 else -1.0) * daubechies[7 - k] for k in range(8)]
    return [(lowpass, highpass), (lowpass[::-1], highpass[::-1])]


def bank_matrix(length):
    half = length // 2
    out = np.zeros((2, 2, half, length))
    rows = np.arange(half)
    for tree, pair in enumerate(filter_bank()):
        for band, taps in enumerate(pair):
            for k in range(8):
                np.add.at(out[tree, band], (rows, (2 * rows + k - 3) % length), taps[k])
    return out.reshape(2, length, length)


def halves(matrix):
    m32 = np.asarray(matrix, np.float32)
    hi = m32.astype(jnp.bfloat16)
    lo = (m32 - hi.astype(np.float32)).astype(jnp.bfloat16)
    return np.stack([hi, lo])


def dft_table():
    t = np.arange(N)
    f = np.arange(BINS)
    phases = ((t[:, None] * f[None, :]) % N).astype(np.float64) * (2.0 * math.pi / N)
    table = np.concatenate([np.cos(phases), -np.sin(phases)], 1)
    return table.astype(np.float32).astype(jnp.bfloat16)


def split(x):
    hi = x.astype(jnp.bfloat16)
    lo = (x - hi.astype(jnp.float32)).astype(jnp.bfloat16)
    return hi, lo


def dot(a, b, trans_b):
    dims = (((1,), (1 if trans_b else 0,)), ((), ()))
    return lax.dot_general(a, b, dims, preferred_element_type=jnp.float32)


def dot3(a, b, trans_b=False):
    return dot(a[0], b[0], trans_b) + (dot(a[1], b[0], trans_b) + dot(a[0], b[1], trans_b))


def greet_all():
    n_tm = lax.axis_size("tm")
    n = lax.axis_size("chan") * n_tm
    me = lax.axis_index("chan") * n_tm + lax.axis_index("tm")
    barrier = pltpu.get_barrier_semaphore()

    def greet(k, carry):
        d = lax.rem(me + k, n)
        pl.semaphore_signal(
            barrier, inc=1, device_id=(d // n_tm, lax.rem(d, n_tm)), device_id_type=MESH
        )
        return carry

    lax.fori_loop(1, n, greet, 0)
    pl.semaphore_wait(barrier, n - 1)


def gather(
    samples, slab, rim_slab, blocks, rims, edge, send, recv, edge_send, edge_recv
):
    n_chan, n_tm = lax.axis_size("chan"), lax.axis_size("tm")
    c, t = lax.axis_index("chan"), lax.axis_index("tm")
    rows, width = samples.shape
    count = width // BLOCK
    rep = n_chan // count
    values = samples[...]
    for j in range(count):
        right, left = (BLOCK * (j + 1)) % width, (BLOCK * j - HALF) % width
        blocks[j] = values[:, BLOCK * j : BLOCK * (j + 1)]
        rims[j] = jnp.concatenate(
            [values[:, right : right + HALF], values[:, left : left + HALF]], 1
        ).astype(jnp.bfloat16)
    rims[count] = jnp.concatenate([values[:, :HALF], values[:, width - HALF :]], 1).astype(
        jnp.bfloat16
    )
    greet_all()
    mine = pl.ds(pl.multiple_of(c * rows, rows), rows)
    place = c // rep

    def pair(to, rows_at, landing):
        return (
            pltpu.make_async_remote_copy(
                src_ref=blocks.at[to // rep],
                dst_ref=slab.at[rows_at, :],
                send_sem=send.at[to],
                recv_sem=recv.at[landing],
                device_id=(to, t),
                device_id_type=MESH,
            ),
            pltpu.make_async_remote_copy(
                src_ref=rims.at[to // rep],
                dst_ref=rim_slab.at[rows_at, :],
                send_sem=send.at[n_chan + to],
                recv_sem=recv.at[n_chan + landing],
                device_id=(to, t),
                device_id_type=MESH,
            ),
        )

    def remote(to):
        return pair(to, mine, c)

    def incoming(source):
        return pair(source, pl.ds(pl.multiple_of(source * rows, rows), rows), source)

    def rim(to, shift, r):
        return pltpu.make_async_remote_copy(
            src_ref=rims.at[count],
            dst_ref=edge.at[mine, :],
            send_sem=edge_send.at[r],
            recv_sem=edge_recv.at[c],
            device_id=(to, lax.rem(t + shift, n_tm)),
            device_id_type=MESH,
        )

    for r in range(rep):
        rim(r, 1, r).start()
        rim((count - 1) * rep + r, n_tm - 1, rep + r).start()
    slab[mine, :] = blocks[place]
    rim_slab[mine, :] = rims[place]

    def start(k, carry):
        for copy in remote(lax.rem(c + k, n_chan)):
            copy.start()
        return carry

    lax.fori_loop(1, n_chan, start, 0)

    def finish(k, carry):
        for copy in incoming(lax.rem(c + n_chan - k, n_chan)):
            copy.wait_recv()
        return carry

    lax.fori_loop(1, n_chan, finish, 0)
    at_edge = jnp.logical_or(place == 0, place == count - 1)

    @pl.when(at_edge)
    def _():
        def take(source, carry):
            pltpu.make_async_remote_copy(
                src_ref=rims.at[count],
                dst_ref=edge.at[pl.ds(pl.multiple_of(source * rows, rows), rows), :],
                send_sem=edge_send.at[0],
                recv_sem=edge_recv.at[source],
                device_id=(source, lax.rem(t + 1, n_tm)),
                device_id_type=MESH,
            ).wait_recv()
            return carry

        lax.fori_loop(0, n_chan, take, 0)

    left = lax.broadcasted_iota(jnp.int32, edge.shape, 1) < HALF

    @pl.when(place == 0)
    def _():
        rim_slab[...] = jnp.where(left, rim_slab[...], edge[...])

    @pl.when(place == count - 1)
    def _():
        rim_slab[...] = jnp.where(left, edge[...], rim_slab[...])

    def sent(k, carry):
        for copy in remote(lax.rem(c + k, n_chan)):
            copy.wait_send()
        return carry

    lax.fori_loop(1, n_chan, sent, 0)
    for r in range(rep):
        rim(r, 1, r).wait_send()
        rim((count - 1) * rep + r, n_tm - 1, rep + r).wait_send()


def shrink(aa, ab, ba, bb, cut_one, cut_two):
    root_half = 1.0 / math.sqrt(2.0)
    re1 = (aa - bb) * root_half
    im1 = (ab + ba) * root_half
    re2 = (aa + bb) * root_half
    im2 = (ab - ba) * root_half
    f1 = jnp.maximum(1.0 - cut_one * lax.rsqrt(re1 * re1 + im1 * im1), 0.0) * root_half
    f2 = jnp.maximum(1.0 - cut_two * lax.rsqrt(re2 * re2 + im2 * im2), 0.0) * root_half
    re1, im1, re2, im2 = re1 * f1, im1 * f1, re2 * f2, im2 * f2
    return re1 + re2, im1 + im2, im1 - im2, re2 - re1


def cut_maps(cuts, level, shape, low_rows, low_cols):
    row_low = lax.broadcasted_iota(jnp.int32, shape, 0) < low_rows
    col_low = lax.broadcasted_iota(jnp.int32, shape, 1) < low_cols
    pick = []
    for k in range(2):
        lh, hl, hh = (cuts[level, 2 * o + k].astype(jnp.float32) / 32.0 for o in range(3))
        pick.append(jnp.where(row_low, lh, jnp.where(col_low, hl, hh)))
    return pick[0], pick[1], jnp.logical_and(row_low, col_low)


def packed(matrix):
    hi, lo = halves(matrix)
    return np.concatenate(
        [np.concatenate([hi, hi], -1), np.concatenate([lo, np.zeros_like(lo)], -1)], -2
    )


def by_rows(x, weight):
    y = dot(jnp.concatenate(split(x), 1), weight, True)
    half = weight.shape[0] // 2
    return y[:, :half] + y[:, half:]


def by_cols(weight, x):
    y = dot(weight, jnp.concatenate(split(x), 0), False)
    half = weight.shape[0] // 2
    return y[:half] + y[half:]


def both_ways(bands, chan_weight, time_weight):
    rows, cols = bands[0].shape
    timed = []
    for q in range(2):
        timed.append(by_rows(jnp.concatenate([bands[q], bands[2 + q]], 0), time_weight[q]))
    out = []
    for p in range(2):
        part = slice(p * rows, (p + 1) * rows)
        y = by_cols(chan_weight[p], jnp.concatenate([timed[0][part], timed[1][part]], 1))
        out += [y[:, :cols], y[:, cols:]]
    return out


def denoise(cuts, slab, rim_slab, sources, tables, picked, cleaned, coefs):
    c1, c1t, t1, c2, c2t, t2, t2t, c3, c3t, t3, t3t = tables
    trees = [(0, 0), (0, 1), (1, 0), (1, 1)]
    rows = slab.shape[0]
    cols = 2 * BLOCK
    hi, lo = split(slab[...])
    rim = rim_slab[...]
    x = jnp.concatenate([hi, rim], 1), jnp.concatenate([lo, jnp.zeros_like(rim)], 1)
    first = split(dot3(x, (t1[0], t1[1]), True))
    coefs[...] = dot3((c1[0], c1[1]), first)
    hr, hc = rows // 2, cols // 2
    corners = [
        (slice(p * rows, p * rows + hr), slice(q * cols, q * cols + hc)) for p, q in trees
    ]
    lows = both_ways([coefs[a, b] for a, b in corners], c2, t2)
    deep = both_ways(lows, c3, t3)
    live = hr // 2
    deep = [band[:live] for band in deep]
    one, two, kept = cut_maps(cuts, 2, deep[0].shape, hr // 4, hc // 4)
    shrunk = shrink(*deep, one, two)
    deep = [jnp.where(kept, a, b) for a, b in zip(deep, shrunk)]
    rest = jnp.zeros((hr - live, hc), jnp.float32)
    inner = both_ways([jnp.concatenate([band, rest], 0) for band in deep], c3t, t3t)
    one, two, kept = cut_maps(cuts, 1, lows[0].shape, hr // 2, hc // 2)
    shrunk = shrink(*lows, one, two)
    outer = both_ways([jnp.where(kept, a, b) for a, b in zip(inner, shrunk)], c2t, t2t)
    for orient, (row_high, col_high) in enumerate([(0, 1), (1, 0), (1, 1)]):
        spots = [
            (
                slice(p * rows + row_high * hr, p * rows + row_high * hr + hr),
                slice(q * cols + col_high * hc, q * cols + col_high * hc + hc),
            )
            for p, q in trees
        ]
        top = [
            cuts[0, 2 * orient + k].astype(jnp.float32) / 32.0 for k in range(2)
        ]
        done = shrink(*[coefs[a, b] for a, b in spots], top[0], top[1])
        for (a, b), cell in zip(spots, done):
            coefs[a, b] = cell
    for (a, b), band in zip(corners, outer):
        coefs[a, b] = band
    hi, lo = split(coefs[...])
    t_hi, t_lo = t1[0, :, :BLOCK], t1[1, :, :BLOCK]
    y = dot(hi, jnp.concatenate([t_hi, t_lo], 1), False)
    timed = jnp.concatenate(split(y[:, :BLOCK] + y[:, BLOCK:] + dot(lo, t_hi, False)), 1)
    y = dot(c1t[0], timed, False)
    whole = y[:, :BLOCK] + y[:, BLOCK:] + dot(c1t[1], timed[:, :BLOCK], False)
    result = (0.25 * whole).astype(jnp.bfloat16)
    cleaned[...] = result.astype(jnp.float32).reshape(rows // 8, 8, BLOCK).astype(jnp.bfloat16)
    one_hot = jnp.where(
        lax.broadcasted_iota(jnp.int32, (rows, sources.shape[1]), 0) == sources[...], 1.0, 0.0
    )
    chosen = jnp.transpose(one_hot).astype(jnp.bfloat16)
    picked[...] = dot(chosen, result, False).astype(jnp.bfloat16)


def spread(picks, cleaned, receivers, near, far, across, recv, send, land, own):
    n_chan, n_tm = lax.axis_size("chan"), lax.axis_size("tm")
    c, t = lax.axis_index("chan"), lax.axis_index("tm")
    blocks = picks.shape[0]
    count = blocks // n_tm
    rep = n_chan // count
    pairs = n_tm // 2
    share = cleaned.shape[0] * 8 // (n_chan * n_tm)
    place, copy_index, core = c // rep, lax.rem(c, rep), lax.rem(t, 2)
    mine = t * count + place

    def move(block, sem, chan, tm):
        return pltpu.make_async_remote_copy(
            src_ref=picks.at[block],
            dst_ref=picks.at[block],
            send_sem=sem,
            recv_sem=recv.at[block],
            device_id=(chan, tm),
            device_id_type=MESH,
        )

    def group(k):
        return move(mine, near.at[k], lax.rem(place + k, count) * rep + copy_index, t)

    def along(u, k):
        to = lax.rem(t // 2 + u, pairs) * 2 + core
        chan = lax.rem(place + k, count) * rep + copy_index
        return move(mine, far.at[u * count + k], chan, to)

    def beside(u, k):
        other = lax.rem(t // 2 + pairs - u, pairs) * 2 + core
        block = other * count + lax.rem(place + count - k, count)
        return move(block, across.at[u * count + k], c, t + 1 - 2 * core)

    def rows_of(dc, dt):
        return (dc * n_tm + dt) * share // 8

    def personal(k):
        dc = lax.rem(place + k // n_tm, count) * rep + copy_index
        dt = lax.rem(t + lax.rem(k, n_tm), n_tm)
        return pltpu.make_async_remote_copy(
            src_ref=cleaned.at[rows_of(dc, dt)],
            dst_ref=receivers.at[mine],
            send_sem=send.at[k],
            recv_sem=land.at[mine],
            device_id=(dc, dt),
            device_id_type=MESH,
        )

    def each(low, high, act):
        def body(k, carry):
            act(k)
            return carry

        lax.fori_loop(low, high, body, 0)

    def await_block(block):
        move(block, near.at[0], c, t + 1 - 2 * core).wait_recv()

    def relay(k):
        @pl.when(k > 0)
        def _():
            await_block(t * count + lax.rem(place + count - k, count))

        beside(0, k).start()

    each(1, count, lambda k: group(k).start())
    for u in range(1, pairs):
        each(0, count, lambda k, u=u: along(u, k).start())
    local = pltpu.make_async_copy(cleaned.at[rows_of(c, t)], receivers.at[mine], own)
    local.start()
    relay(0)
    each(1, blocks, lambda k: personal(k).start())
    each(1, count, relay)
    for u in range(1, pairs):

        def cross_over(k, u=u):
            other = lax.rem(t // 2 + pairs - u, pairs) * 2 + core
            await_block(other * count + lax.rem(place + count - k, count))
            beside(u, k).start()

        each(0, count, cross_over)
    for u in range(pairs):

        def last(k, u=u):
            other = lax.rem(t // 2 + pairs - u, pairs) * 2 + 1 - core
            await_block(other * count + lax.rem(place + count - k, count))

        each(0, count, last)

    def landed(k):
        block = lax.rem(mine + k, blocks)
        pltpu.make_async_remote_copy(
            src_ref=cleaned.at[0],
            dst_ref=receivers.at[block],
            send_sem=send.at[0],
            recv_sem=land.at[block],
            device_id=(c, t + 1 - 2 * core),
            device_id_type=MESH,
        ).wait_recv()

    local.wait()
    each(1, blocks, landed)
    each(1, count, lambda k: group(k).wait_send())
    each(1, blocks, lambda k: personal(k).wait_send())
    for u in range(pairs):
        each(0, count, lambda k, u=u: beside(u, k).wait_send())
        if u:
            each(0, count, lambda k, u=u: along(u, k).wait_send())


def whole_kernel(n_tables, same, cuts, samples, sources, *refs):
    stored, refs = refs[:n_tables], refs[n_tables:]
    out, picks, receivers, white, heard, cross = refs[:6]
    held, refs = refs[6 : 6 + n_tables], refs[6 + n_tables :]
    slab, rim_slab, blocks, rims, edge, coefs, cleaned, loads = refs[:8]
    gather_sems, spread_sems = refs[8:12], refs[12:]
    copies = [pltpu.make_async_copy(a, b, loads.at[i]) for i, (a, b) in enumerate(zip(stored, held))]
    for copy in copies:
        copy.start()
    gather(samples, slab, rim_slab, blocks, rims, edge, *gather_sems)
    for copy in copies[:-1]:
        copy.wait()
    c1t, t1, c2, c2t, c3, c3t = held[:6]
    extra = [t1, c2, c2t, c3, c3t] if same else held[6:-1]
    tables = [extra[0], c1t, t1, extra[1], extra[2], c2, c2t, extra[3], extra[4], c3, c3t]
    n_tm = lax.axis_size("tm")
    count = picks.shape[0] // n_tm
    rep = lax.axis_size("chan") // count
    mine = lax.axis_index("tm") * count + lax.axis_index("chan") // rep
    denoise(cuts, slab, rim_slab, sources, tables, picks.at[mine], cleaned, coefs)
    spread(picks, cleaned, receivers, *spread_sems)
    copies[-1].wait()
    correlate(picks, receivers, held[-1], out, white, heard, cross)


def correlate(picks, receivers, table, out, white, heard, cross):
    per_window = N // BLOCK
    windows, sources = picks.shape[0] // per_window, picks.shape[1]

    def window(ref, w):
        return jnp.concatenate([ref[w * per_window + j] for j in range(per_window)], 1)

    def whiten(block):
        spectra = dot(block, table[...], False)
        scale = lax.rsqrt(jnp.mean(spectra * spectra, axis=1, keepdims=True) + 1e-05)
        return (spectra * scale).astype(jnp.bfloat16).astype(jnp.float32)

    heard_rows = [window(receivers, w).astype(jnp.float32) for w in range(windows)]
    joined = jnp.concatenate(
        [window(picks, w) for w in range(windows)]
        + [jnp.concatenate(heard_rows, 0).astype(jnp.bfloat16)],
        0,
    )
    spectra = whiten(joined)
    base = windows * sources
    for part in range(N // BLOCK):
        white[part] = spectra[:base, BLOCK * part : BLOCK * (part + 1)]
    for w in range(windows):
        heard[w] = spectra[base + 8 * w : base + 8 * w + 8]
    weight = jnp.where(lax.broadcasted_iota(jnp.int32, (1, BLOCK), 1) == 0, 1.0, 2.0)

    def body(g, carry):
        for chunk in range(BINS // BLOCK):
            lo = chunk * BLOCK
            hi = BINS + lo
            real = [None, None]
            imag = [None, None]
            for w in range(windows):
                rr = heard[w, :, lo : lo + BLOCK]
                ri = heard[w, :, hi : hi + BLOCK]
                for j in range(2):
                    spread = pl.ds(w * sources + 2 * g + j, 8, stride=0)
                    pr = white.at[chunk][spread, :]
                    pi = white.at[chunk + BINS // BLOCK][spread, :]
                    a = pr * rr + pi * ri
                    b = pi * rr - pr * ri
                    real[j] = a if real[j] is None else real[j] + a
                    imag[j] = b if imag[j] is None else imag[j] + b
            factor = weight if chunk == 0 else 2.0
            spot = pl.ds(pl.multiple_of(16 * g, 16), 16)
            cross[spot, lo : lo + BLOCK] = (jnp.concatenate(real, 0) * factor).astype(jnp.bfloat16)
            cross[spot, hi : hi + BLOCK] = (jnp.concatenate(imag, 0) * factor).astype(jnp.bfloat16)
        return carry

    lax.fori_loop(0, sources // 2, body, 0)
    scale = 1.0 / math.sqrt(windows * N)
    half = LAGS // 2
    lags = jnp.concatenate([table[N - half :, :], table[:half, :]], 0)
    out[...] = dot(cross[...], lags, True) * scale


def local(samples, thresholds, sources):
    n_chan, n_tm = lax.axis_size("chan"), lax.axis_size("tm")
    rows, width = samples.shape
    channels = rows * n_chan
    count = width // BLOCK
    rep = n_chan // count
    blocks = count * n_tm
    windows = n_tm * width // N
    picked_count = sources.shape[0]
    vmem = pl.BlockSpec(memory_space=pltpu.VMEM)
    smem = pl.BlockSpec(memory_space=pltpu.SMEM)
    dma = pltpu.SemaphoreType.DMA
    f32, bf16 = jnp.float32, jnp.bfloat16
    big = 60 * 1024 * 1024

    def wide(matrix):
        return halves(matrix.reshape(-1, matrix.shape[-1]))

    def flipped(matrix):
        return np.swapaxes(matrix, -1, -2)

    def cornered(matrix):
        size = matrix.shape[-1]
        return np.pad(matrix, ((0, 0), (0, size), (0, size)))

    def pack_pair(length):
        second, third = bank_matrix(length // 2), cornered(bank_matrix(length // 4))
        return [packed(m) for m in (second, flipped(second), third, flipped(third))]

    same = channels == 2 * BLOCK
    c1, t1 = wide(bank_matrix(channels)), wide(bank_matrix(2 * BLOCK))
    chan, time = pack_pair(channels), pack_pair(2 * BLOCK)
    tables = [np.ascontiguousarray(flipped(c1)), t1, *time]
    if not same:
        tables += [c1, *chan]
    tables.append(dft_table())

    far_count = blocks // 2
    out = pl.pallas_call(
        functools.partial(whole_kernel, len(tables), same),
        out_shape=jax.ShapeDtypeStruct((picked_count * 8, LAGS), f32),
        in_specs=[smem, vmem, vmem] + [pl.BlockSpec(memory_space=pl.ANY)] * len(tables),
        out_specs=vmem,
        scratch_shapes=[
            pltpu.VMEM((blocks, picked_count, BLOCK), bf16),
            pltpu.VMEM((blocks, 8, BLOCK), bf16),
            pltpu.VMEM((N // BLOCK, windows * picked_count, BLOCK), f32),
            pltpu.VMEM((windows, 8, N), f32),
            pltpu.VMEM((picked_count * 8, N), bf16),
        ]
        + [pltpu.VMEM(a.shape, bf16) for a in tables]
        + [
            pltpu.VMEM((channels, BLOCK), f32),
            pltpu.VMEM((channels, BLOCK), bf16),
            pltpu.VMEM((count, rows, BLOCK), f32),
            pltpu.VMEM((count + 1, rows, BLOCK), bf16),
            pltpu.VMEM((channels, BLOCK), bf16),
            pltpu.VMEM((2 * channels, 4 * BLOCK), f32),
            pltpu.VMEM((channels // 8, 8, BLOCK), bf16),
            dma((len(tables),)),
            dma((2 * n_chan,)),
            dma((2 * n_chan,)),
            dma((2 * rep,)),
            dma((n_chan,)),
            dma((count,)),
            dma((far_count,)),
            dma((far_count,)),
            dma((blocks,)),
            dma((blocks,)),
            dma((blocks,)),
            dma,
        ],
        compiler_params=pltpu.CompilerParams(
            collective_id=0, has_side_effects=True, vmem_limit_bytes=big
        ),
        name="whole",
    )(thresholds, samples, sources[None, :], *[jnp.asarray(a) for a in tables])

    out = out.reshape(picked_count, 8, LAGS)
    share = channels // (n_chan * n_tm)
    if share < 8:
        place = lax.axis_index("chan") * n_tm + lax.axis_index("tm")
        out = lax.dynamic_slice_in_dim(out, lax.rem(place * share, 8), share, 1)
    return out


def solution(mesh):
    return jax.shard_map(
        local,
        mesh=mesh,
        in_specs=(P("chan", "tm"), P(), P()),
        out_specs=P(None, ("chan", "tm"), None),
        check_vma=False,
    )
```
